32 devices in a mesh: prow: 4 (over z), pcol: 8 (over y, x, core).
Axes of the slice: x: 2, y: 2, z: 4, core: 2. Of those that a mesh axis runs over, the one named last changes fastest.
Arguments:
- blocks: bfloat16 [2048, 64, 128], P(('prow', 'pcol')), may hold values from -6 to 6
- owner: int32 [2048, 1], P(('prow', 'pcol')), may hold values from 0 to 31; in each aligned block of 64 rows (0 to 63, 64 to 127, ...) at most 2 rows name the same one
- row_offset: int32 [2048], P(('prow', 'pcol')), may hold values from 0 to 320
- col_offset: int32 [2048], P(('prow', 'pcol')), may hold values from 0 to 256
- exposure: int32 [2048], P(('prow', 'pcol')), may hold values from 0 to 255
- basis_rows: bfloat16 [21, 31], replicated, may hold values from -1 to 1
- basis_cols: bfloat16 [21, 31], replicated, may hold values from -1 to 1
- coef_table: float32 [256, 21], replicated, may hold values from -1.25 to 1.25
- weight_table: float32 [256], replicated, may hold values from 0.2 to 2
- det_taps: float32 [31], replicated, may hold values from 0.02 to 0.12
Outputs:
- coadd: float32 [1536, 3072], P('prow', 'pcol')
- detection: float32 [1536, 3072], P('prow', 'pcol')
The draws below stay inside these ranges and needn't reach their ends.
Inputs may be any that keep to these rules, and one draw needn't show every extreme that they name: The blocks of one device name one owner at most 2 times; some device names some owner exactly 2 times.
All inputs are finite; a program needn't handle non-finite values.
Results may differ from the reference program's by a relative error of at most 0.009.
Values may be sent and summed in bfloat16 or wider, within the bound.
A program may use at most 192 MiB of HBM per device.

```python
import math
import jax
import jax.numpy as jnp
import numpy as np
from jax import lax

BASIS = 21
TAPS = 31
DET_R = 15
BH = 64
BW = 128
PATCH = 384
NB = 64
CAP = 2
NTAB = 256
NDEV = 32
TOTAL_BLOCKS = 2048
NX = 1536
NY = 3072
N_PCOL = 8


def plant(values, key, smallest, top_value):
    index_at = [jax.random.randint(jax.random.fold_in(key, axis), (), 0, length) for axis, length in enumerate(values.shape)]
    longest = values.shape.index(max(values.shape))
    beside = index_at[:longest] + [(index_at[longest] + 1) % values.shape[longest]] + index_at[longest + 1:]
    return values.at[tuple(index_at)].set(smallest).at[tuple(beside)].set(top_value)


def block_levels(own_key, shape, cuts, least, top_value):
    def one(dim, parts):
        steps = jax.random.uniform(jax.random.fold_in(jax.random.fold_in(own_key, 6), dim), (parts,), jnp.float32, least / len(cuts), top_value / len(cuts))
        return jnp.repeat(jnp.exp(steps), shape[dim] // parts).reshape((-1,) + (1,) * (len(shape) - dim - 1))

    level = one(*cuts[0])
    for cut in cuts[1:]:
        level = level * one(*cut)
    return level


def shared_out(stream_key, own, number, rows, count, top, most, skew):
    ranking = jax.random.permutation(stream_key, count)
    crowded, common = shares(count, rows * top, most, skew, True), shares(count, rows * top, most, skew, False)
    places = jnp.arange(count)

    def named(lengths, turn):
        used = int((lengths > 0).sum())
        fixed = max(1, used // 4)
        moved = fixed + (places - fixed + turn * (used - fixed)) % max(1, count - fixed)
        return jnp.zeros((count,), jnp.int32).at[ranking[jnp.where(places < fixed, places, moved)]].set(jnp.asarray(lengths, jnp.int32))

    lengths = jnp.where(number % 4 == 0, named(crowded, number // 4), named(common, number - number // 4 - 1))
    mixed = jax.random.permutation(jax.random.fold_in(own, 3), count)
    donor, sink = mixed[0:count // 2 * 2:2], mixed[1:count // 2 * 2:2]
    margin = jnp.minimum(lengths[donor] - 1, most - lengths[sink]) // 2
    margin = jnp.where((donor == ranking[0]) | (sink == ranking[0]) | (lengths[sink] == 0), 0, jnp.maximum(margin, 0))
    moved = jax.random.randint(jax.random.fold_in(own, 4), (count // 2,), 0, 1 << 20) % (margin + 1)
    lengths = lengths.at[donor].add(-moved).at[sink].add(moved)
    labels = jnp.searchsorted(jnp.cumsum(lengths), jnp.arange(rows * top), side="right").astype(jnp.int32)
    table = labels.reshape(top, rows).T
    table = table[jax.random.permutation(jax.random.fold_in(own, 1), rows)]
    turn = jax.random.randint(jax.random.fold_in(own, 2), (rows, 1), 0, top)
    return jnp.take_along_axis(table, (jnp.arange(top)[None, :] + turn) % top, axis=1)


def shares(number_of, total, bound, skew, full):
    loads = [(1 << 20) // math.isqrt(grade ** skew) + 1 for grade in range(1, number_of + 1)]
    largest = bound if full else min(bound, max(-(-total // number_of), total * loads[0] // sum(loads)))
    least = 1 if total - largest >= number_of - 1 else 0
    counts, spare = [largest] + [least] * (number_of - 1), total - largest - least * (number_of - 1)
    while spare > 0:
        candidates = [i for i in range(1, number_of) if counts[i] < largest] or [i for i in range(1, number_of) if counts[i] < bound]
        pool, left = sum([loads[i] for i in candidates]), spare
        for i in candidates:
            more = min(bound - counts[i], max(1, left * loads[i] // pool), spare)
            counts[i] = counts[i] + more
            spare = spare - more
    return np.array(counts)


def noise(key, extent, deviation, most, pieces=(), dtype=jnp.bfloat16):
    gain = block_levels(key, extent, pieces, -0.22, 0.18) if pieces else 1.0
    result = jax.random.normal(key, extent, jnp.float32) * deviation * gain
    return jnp.minimum(jnp.maximum(result, -most), most).astype(dtype)


def setup_inputs(seed: int = 0) -> dict:
    streams_of = jax.random.split(jax.random.key(seed), 11)
    blocks = noise(streams_of[0], (TOTAL_BLOCKS, BH, BW), 1.0, 6.0, ((0, 32),))
    owner_keys = jax.random.split(jax.random.fold_in(streams_of[1], 1), TOTAL_BLOCKS // NB)
    owner_turns = jax.random.permutation(jax.random.fold_in(streams_of[1], 3), TOTAL_BLOCKS // NB)
    owner = jax.vmap(lambda own, number: shared_out(jax.random.fold_in(streams_of[1], 2), own, number, NB, NDEV, 1, CAP, 2))(owner_keys, owner_turns).reshape((TOTAL_BLOCKS, 1))
    row_offset = plant(jax.random.randint(streams_of[2], (TOTAL_BLOCKS,), 0, PATCH - BH + 1), jax.random.fold_in(streams_of[2], 1), 0, PATCH - BH).astype(jnp.int32)
    col_offset = plant(jax.random.randint(streams_of[3], (TOTAL_BLOCKS,), 0, PATCH - BW + 1), jax.random.fold_in(streams_of[3], 1), 0, PATCH - BW).astype(jnp.int32)
    exposure = plant(jax.random.randint(streams_of[4], (TOTAL_BLOCKS,), 0, NTAB), jax.random.fold_in(streams_of[4], 1), 0, NTAB - 1).astype(jnp.int32)
    basis_rows = noise(streams_of[5], (BASIS, TAPS), TAPS ** -0.5, 1.0)
    basis_cols = noise(streams_of[6], (BASIS, TAPS), TAPS ** -0.5, 1.0)
    coef_table = noise(streams_of[7], (NTAB, BASIS), BASIS ** -0.5, 1.25, (), jnp.float32)
    weight_table = jnp.clip(jnp.exp(jax.random.uniform(streams_of[8], (NTAB,), jnp.float32, math.log(0.2), math.log(2.0))), 0.2, 2.0)
    det_taps = jnp.clip(jax.random.uniform(streams_of[9], (2 * DET_R + 1,), jnp.float32, 0.02, 0.12), 0.02, 0.12)
    return dict(blocks=blocks, owner=owner, row_offset=row_offset, col_offset=col_offset, exposure=exposure, basis_rows=basis_rows, basis_cols=basis_cols, coef_table=coef_table, weight_table=weight_table, det_taps=det_taps)


def match_group(pixels, coefs, basis_rows, basis_cols):
    half = TAPS // 2
    taps = jnp.arange(TAPS)
    cols_in = jnp.arange(BW)
    rows_in = jnp.arange(BH)
    col_hits = ((cols_in[:, None, None] - cols_in[None, :, None] + half) == taps[None, None, :]).astype(jnp.float32)
    col_table = jnp.einsum('bct,kt->bkc', col_hits, basis_cols.astype(jnp.float32))
    section = jnp.einsum('gab,bkc->gakc', pixels.astype(jnp.float32), col_table).astype(jnp.bfloat16)
    scaled = (coefs[:, :, None] * basis_rows.astype(jnp.float32)[None]).astype(jnp.bfloat16)
    row_hits = ((rows_in[None, :, None] - rows_in[:, None, None] + half) == taps[None, None, :]).astype(jnp.float32)
    row_table = jnp.einsum('rat,gkt->grka', row_hits, scaled.astype(jnp.float32))
    return jnp.einsum('grka,gakc->grc', row_table, section.astype(jnp.float32)).astype(jnp.bfloat16)


def reference(blocks, owner, row_offset, col_offset, exposure, basis_rows, basis_cols, coef_table, weight_table, det_taps):
    group = 64
    count = blocks.shape[0]
    while count % group != 0:
        group = group // 2
    coefs = coef_table[exposure]
    weights = weight_table[exposure].astype(jnp.bfloat16).astype(jnp.float32)

    def one(args):
        pixels, coef, weight = args
        matched = match_group(pixels, coef, basis_rows, basis_cols)
        return (weight[:, None, None] * matched.astype(jnp.float32)).astype(jnp.bfloat16)

    weighted = lax.map(one, (blocks.reshape(count // group, group, BH, BW), coefs.reshape(count // group, group, BASIS), weights.reshape(count // group, group)))
    weighted = weighted.reshape(count, BH, BW)
    dest = owner[:, 0].astype(jnp.int32)
    top_rows = ((dest // N_PCOL) * PATCH + row_offset).astype(jnp.int32)
    left_cols = ((dest % N_PCOL) * PATCH + col_offset).astype(jnp.int32)

    def place(index, carry):
        total, depth = carry
        here_row = top_rows[index]
        here_col = left_cols[index]
        old = lax.dynamic_slice(total, (here_row, here_col), (BH, BW))
        total = lax.dynamic_update_slice(total, old + weighted[index].astype(jnp.float32), (here_row, here_col))
        old_depth = lax.dynamic_slice(depth, (here_row, here_col), (BH, BW))
        depth = lax.dynamic_update_slice(depth, old_depth + weights[index], (here_row, here_col))
        return (total, depth)

    start = (jnp.zeros((NX, NY), jnp.float32), jnp.zeros((NX, NY), jnp.float32))
    total, depth = lax.fori_loop(0, count, place, start)
    coadd = total / jnp.maximum(depth, 1.0)
    padded = jnp.pad(coadd, DET_R)
    across = jnp.zeros((NX, NY + 2 * DET_R), jnp.float32)
    for step in range(2 * DET_R + 1):
        across = across + det_taps[step] * padded[step:step + NX, :]
    detection = jnp.zeros((NX, NY), jnp.float32)
    for step in range(2 * DET_R + 1):
        detection = detection + det_taps[step] * across[:, step:step + NY]
    return coadd, detection
```

```python
import functools

import jax
import jax.numpy as jnp
from jax import lax
from jax.experimental import pallas as pl
from jax.experimental.pallas import tpu as pltpu
from jax.sharding import PartitionSpec as P

DET_R = 15
PATCH = 384
CAP = 2
LANES = 128
MESH = pl.DeviceIdType.MESH
EXACT = lax.Precision.HIGHEST


HALO = 16
MGROUP = 4
WIDE = 512


def split_dot(left, right, dims):
    def parts(value):
        high = value.astype(jnp.bfloat16)
        return high, (value - high.astype(jnp.float32)).astype(jnp.bfloat16)

    (a, b), (c, d) = parts(left), parts(right)
    dot = functools.partial(
        lax.dot_general, dimension_numbers=(dims, ((), ())), preferred_element_type=jnp.float32
    )
    return dot(a, c) + (dot(a, d) + dot(b, c))


def prepare(kinds, ncol, owner, exposure, row_offset, col_offset, weights, coef_table, picks_out, told_out, coef_out):
    count = owner.shape[1]
    entries = weights.shape[1]
    slots = coef_out.shape[0]
    owners = slots // CAP
    at_sub = lax.broadcasted_iota(jnp.int32, (count, count), 0)
    at_lane = lax.broadcasted_iota(jnp.int32, (count, count), 1)

    def column(row):
        spread = jnp.broadcast_to(row, (count, count))
        return jnp.sum(jnp.where(at_sub == at_lane, spread, 0), axis=1, keepdims=True)

    same = jnp.where((column(owner[...]) == owner[...]) & (at_sub < at_lane), 1, 0)
    slot = owner[...] * CAP + jnp.sum(same, axis=0, keepdims=True)
    at_slot = lax.broadcasted_iota(jnp.int32, (count, slots), 1) == column(slot)
    numbers = lax.broadcasted_iota(jnp.int32, (count, slots), 0)
    picks_out[...] = jnp.sum(jnp.where(at_slot, numbers, 0), axis=0, keepdims=True)
    lane = lax.broadcasted_iota(jnp.int32, (owners, LANES), 1)
    told = jnp.zeros((owners, LANES), jnp.int32)
    for j in range(CAP):
        own = lax.broadcasted_iota(jnp.int32, (owners, count), 0) * CAP + j == slot
        values = (jnp.ones_like(slot), exposure[...], row_offset[...], col_offset[...])
        for n, value in enumerate(values):
            found = jnp.sum(jnp.where(own, value, 0), axis=1, keepdims=True)
            told = jnp.where(lane == 4 * j + n, found, told)
    for o in range(owners):
        told_out[o // ncol, o % ncol] = told[o : o + 1, :]
    own = lax.broadcasted_iota(jnp.int32, (slots, count), 0) == slot
    index = jnp.sum(jnp.where(own, exposure[...], 0), axis=1, keepdims=True)
    hits = lax.broadcasted_iota(jnp.int32, (slots, entries), 1) == index
    weight = jnp.sum(jnp.where(hits, weights[...], 0.0), axis=1, keepdims=True)
    weight = weight.astype(jnp.bfloat16).astype(jnp.float32)
    cols = coef_out.shape[1] // kinds
    coefs = lax.dot_general(
        hits.astype(jnp.float32),
        coef_table[...],
        (((1,), (1,)), ((), ())),
        precision=EXACT,
        preferred_element_type=jnp.float32,
    )
    coefs = coefs * weight
    for k in range(kinds):
        coef_out[:, k * cols : (k + 1) * cols] = jnp.broadcast_to(
            coefs[:, k : k + 1], (slots, cols)
        )


def build_tables(basis_rows, basis_cols, col_out, row_out):
    kinds, taps = basis_rows.shape
    half = taps // 2
    rows, cols = row_out.shape[0], col_out.shape[0]
    tap = lax.broadcasted_iota(jnp.int32, (taps, LANES), 0)
    lane = lax.broadcasted_iota(jnp.int32, (taps, LANES), 1)

    def spread(value, target):
        hot = jnp.where(lane == (target + LANES) % LANES, 1.0, 0.0).astype(jnp.bfloat16)
        return jnp.dot(value[...], hot, preferred_element_type=jnp.float32)

    col_src = spread(basis_cols, half - tap)
    even = spread(basis_rows, tap - half)
    odd = spread(basis_rows, tap - half + rows)
    near = jnp.abs(
        lax.broadcasted_iota(jnp.int32, (cols, LANES), 1)
        - lax.broadcasted_iota(jnp.int32, (cols, LANES), 0)
    )
    for k in range(kinds):
        source = jnp.broadcast_to(col_src[k : k + 1, :], (cols, LANES))
        rolled = pltpu.roll(source, 0, 1, stride=1, stride_axis=0)
        col_out[:, k * LANES : (k + 1) * LANES] = jnp.where(near <= half, rolled, 0.0).astype(
            jnp.bfloat16
        )
    near = jnp.abs(
        lax.broadcasted_iota(jnp.int32, (rows, LANES), 1) % rows
        - lax.broadcasted_iota(jnp.int32, (rows, LANES), 0)
    )
    for k in range(0, kinds, 2):
        source = even[k : k + 1, :]
        if k + 1 < kinds:
            source = source + odd[k + 1 : k + 2, :]
        rolled = pltpu.roll(
            jnp.broadcast_to(source, (rows, LANES)), 0, 1, stride=1, stride_axis=0
        )
        row_out[:, k * rows : k * rows + LANES] = jnp.where(near <= half, rolled, 0.0).astype(
            jnp.bfloat16
        )


def whole_kernel(
    nrow,
    ncol,
    owner,
    exposure,
    row_offset,
    col_offset,
    weights,
    coef_table,
    basis_rows,
    basis_cols,
    taps,
    source_blocks,
    coadd,
    detection,
    blocks,
    pick_row,
    picks,
    info,
    coefs,
    col_table,
    row_table,
    sections,
    outgoing,
    arrived,
    relay,
    heard,
    total,
    image,
    halo,
    sems,
    data_sems,
    halo_sems,
    row_sems,
    col_sems,
):
    owners = nrow * ncol
    prow, pcol = lax.axis_index("prow"), lax.axis_index("pcol")
    me = prow * ncol + pcol
    rows, cols = blocks.shape[1:]
    kinds = basis_rows.shape[0]
    span = nrow // 2 if nrow % 2 == 0 else nrow

    def turn(i):
        i = i // 2 + (i % 2) * (owners // 2)
        step, col = i // ncol, (pcol + 1 + i) % ncol
        side = (prow // span + 1 + step // span) % (nrow // span)
        return (side * span + (prow + 1 + step) % span) * ncol + col

    def source(i):
        i = i // 2 + (i % 2) * (owners // 2)
        step, col = i // ncol, (pcol + 2 * ncol - 1 - i % ncol) % ncol
        side = (prow // span + 1 + step // span) % (nrow // span)
        return (side * span + (prow + 2 * span - 1 - step % span) % span) * ncol + col

    def place(device):
        return (device // ncol, device % ncol)

    load = pltpu.make_async_copy(source_blocks, blocks, sems.at[3])
    load.start()
    halo[...] = jnp.zeros_like(halo)
    image[0:HALO, :] = jnp.zeros((HALO, WIDE), jnp.float32)
    image[PATCH + HALO :, :] = jnp.zeros((WIDE - PATCH - HALO, WIDE), jnp.float32)
    barrier = pltpu.get_barrier_semaphore()

    def greet(i, carry):
        other = lax.rem(me + i, owners)
        pl.semaphore_signal(barrier, inc=1, device_id=place(other), device_id_type=MESH)
        return carry

    lax.fori_loop(1, owners, greet, 0)
    prepare(
        kinds, ncol, owner, exposure, row_offset, col_offset, weights, coef_table, pick_row, info, coefs
    )
    lift = pltpu.make_async_copy(pick_row, picks, sems.at[2])
    lift.start()
    build_tables(basis_rows, basis_cols, col_table, row_table)
    total[...] = jnp.zeros_like(total)
    lift.wait()
    load.wait()

    def row_copy(to, origin):
        return pltpu.make_async_remote_copy(
            src_ref=info.at[to],
            dst_ref=relay.at[pl.ds(0, ncol), origin],
            send_sem=row_sems.at[0, to],
            recv_sem=row_sems.at[1, origin],
            device_id=(to, pcol),
            device_id_type=MESH,
        )

    def col_copy(to, origin):
        return pltpu.make_async_remote_copy(
            src_ref=relay.at[to],
            dst_ref=heard.at[origin],
            send_sem=col_sems.at[0, to],
            recv_sem=col_sems.at[1, origin],
            device_id=(prow, to),
            device_id_type=MESH,
        )

    def tell_rows():
        for n in range(1, nrow):
            row_copy(lax.rem(prow + n, nrow), prow).start()
        for c in range(ncol):
            relay[c, prow] = info[prow, c]

    def tell_cols():
        for n in range(1, nrow):
            row = lax.rem(prow + n, nrow)
            row_copy(row, row).wait_recv()
        for n in range(1, ncol):
            col_copy(lax.rem(pcol + n, ncol), pcol).start()
        heard[pcol] = relay[pcol]

    mgroup = MGROUP

    def matched_group(first):
        slots_of = [
            turn(first + n) * CAP + j for n in range(mgroup) for j in range(CAP)
        ]
        pixels = jnp.concatenate([blocks[picks[0, s]] for s in slots_of], axis=0)
        coefs_of = [coefs[pl.ds(s, 1), :] for s in slots_of]
        section = jnp.dot(pixels, col_table[...], preferred_element_type=jnp.float32)
        for k in range(kinds):
            for n, coef in enumerate(coefs_of):
                part = section[n * rows : (n + 1) * rows, k * cols : (k + 1) * cols]
                sections[k * rows : (k + 1) * rows, n * cols : (n + 1) * cols] = (
                    coef[:, k * cols : (k + 1) * cols] * part
                ).astype(jnp.bfloat16)
        matched = jnp.dot(
            row_table[:, 0 : kinds * rows], sections[...], preferred_element_type=jnp.float32
        ).astype(jnp.bfloat16)
        for n in range(mgroup):
            for j in range(CAP):
                m = n * CAP + j
                outgoing[turn(first + n), j * rows : (j + 1) * rows, :] = matched[
                    :, m * cols : (m + 1) * cols
                ]

    def data_copy(other, origin):
        return pltpu.make_async_remote_copy(
            src_ref=outgoing.at[other],
            dst_ref=arrived.at[origin],
            send_sem=data_sems.at[0, other],
            recv_sem=data_sems.at[1, origin],
            device_id=place(other),
            device_id_type=MESH,
        )

    early = 0

    def send(g, carry):
        matched_group(g * mgroup)

        @pl.when(g == early)
        def _():
            pl.semaphore_wait(barrier, owners - 1)
            tell_rows()

            def start(i, carry):
                data_copy(turn(i), me).start()
                return carry

            lax.fori_loop(0, early * mgroup, start, 0)

        @pl.when(g == early + 2)
        def _():
            tell_cols()

        for n in range(mgroup):
            other = turn(g * mgroup + n)

            @pl.when((g >= early) & (g * mgroup + n < owners - 1))
            def _():
                data_copy(other, me).start()

        return carry

    lax.fori_loop(0, owners // mgroup, send, 0)
    arrived[me] = outgoing[me]
    for n in range(1, ncol):
        col = lax.rem(pcol + n, ncol)
        col_copy(col, col).wait_recv()

    wide = lax.broadcasted_iota(jnp.int32, (owners, PATCH), 1)
    entries = weights.shape[1]
    letters = jnp.concatenate([heard[o % ncol, o // ncol] for o in range(owners)], axis=0)
    depth = jnp.zeros((PATCH, PATCH), jnp.float32)
    for j in range(CAP):
        live, entry, top, left = (letters[:, 4 * j + n : 4 * j + n + 1] for n in range(4))
        hits = lax.broadcasted_iota(jnp.int32, (owners, entries), 1) == entry
        weight = jnp.sum(jnp.where(hits, weights[...], 0.0), axis=1, keepdims=True)
        weight = jnp.where(live > 0, weight, 0.0)
        row_weight = jnp.where((wide >= top) & (wide < top + rows), weight, 0.0)
        col_cover = jnp.where((wide >= left) & (wide < left + cols), 1.0, 0.0)
        depth = depth + lax.dot_general(
            row_weight.astype(jnp.bfloat16),
            col_cover.astype(jnp.bfloat16),
            (((0,), (0,)), ((), ())),
            preferred_element_type=jnp.float32,
        )
    coadd[...] = jnp.maximum(depth, 1.0)

    offset = lax.broadcasted_iota(jnp.int32, (cols, PATCH), 1) - lax.broadcasted_iota(
        jnp.int32, (cols, PATCH), 0
    )
    group = 4
    many = group * CAP
    down = lax.broadcasted_iota(jnp.int32, (PATCH, many * rows), 0)
    lane = lax.broadcasted_iota(jnp.int32, (1, many * rows), 1)

    def gather(g, carry):
        target = lane % rows
        shifted = []
        for n in range(group):
            origin = source(g * group + n)

            @pl.when(g * group + n < owners - 1)
            def _():
                data_copy(origin, origin).wait_recv()

            letter = heard[origin % ncol, origin // ncol]
            for j in range(CAP):
                live, _, top, left = (letter[:, 4 * j + n : 4 * j + n + 1] for n in range(4))
                hot = jnp.where((offset == left) & (live > 0), 1.0, 0.0).astype(jnp.bfloat16)
                block = arrived[origin, j * rows : (j + 1) * rows, :]
                shifted.append(
                    jnp.dot(block, hot, preferred_element_type=jnp.float32).astype(jnp.bfloat16)
                )
                target = target + jnp.where(lane // rows == n * CAP + j, top, 0)
        hot = jnp.where(down == target, 1.0, 0.0).astype(jnp.bfloat16)
        total[...] += jnp.dot(
            hot, jnp.concatenate(shifted, axis=0), preferred_element_type=jnp.float32
        )
        return carry

    lax.fori_loop(0, owners // group, gather, 0)
    coadd[...] = total[...] / coadd[...]

    first_rows, last_rows = pl.ds(0, HALO), pl.ds(PATCH - HALO, HALO)
    first, last, whole = pl.ds(0, LANES), pl.ds(PATCH - LANES, LANES), pl.ds(0, PATCH)
    left_tile, right_tile = pl.ds(PATCH, LANES), pl.ds(PATCH + LANES, LANES)
    below = pl.ds(HALO, HALO)
    moves = (
        (1, 0, coadd.at[last_rows, whole], halo.at[first_rows, whole]),
        (-1, 0, coadd.at[first_rows, whole], halo.at[below, whole]),
        (1, 1, coadd.at[last_rows, last], halo.at[first_rows, left_tile]),
        (1, -1, coadd.at[last_rows, first], halo.at[first_rows, right_tile]),
        (-1, 1, coadd.at[first_rows, last], halo.at[below, left_tile]),
        (-1, -1, coadd.at[first_rows, first], halo.at[below, right_tile]),
        (0, -1, image.at[below, whole], image.at[pl.ds(PATCH + HALO, HALO), whole]),
        (0, 1, image.at[pl.ds(PATCH, HALO), whole], image.at[first_rows, whole]),
    )

    def inside(dp, dc):
        row, col = prow + dp, pcol + dc
        return (row >= 0) & (row < nrow) & (col >= 0) & (col < ncol)

    def halo_copy(n):
        dp, dc, origin, target = moves[n]
        return pltpu.make_async_remote_copy(
            src_ref=origin,
            dst_ref=target,
            send_sem=halo_sems.at[0, n],
            recv_sem=halo_sems.at[1, n],
            device_id=(prow + dp, pcol + dc),
            device_id_type=MESH,
        )

    for n, (dp, dc, _, _) in enumerate(moves):
        if dp == 0 and dc < 0:
            image[HALO : HALO + PATCH, 0:PATCH] = coadd[...].T

        @pl.when(inside(dp, dc))
        def _():
            halo_copy(n).start()

    def sent(i, carry):
        other = turn(i)
        data_copy(other, other).wait_send()
        return carry

    lax.fori_loop(0, owners - 1, sent, 0)
    for n in range(1, nrow):
        row_copy(lax.rem(prow + n, nrow), prow).wait_send()
    for n in range(1, ncol):
        col_copy(lax.rem(pcol + n, ncol), pcol).wait_send()

    reach = taps.shape[1]
    at_sub = lax.broadcasted_iota(jnp.int32, (reach, reach), 0)
    at_lane = lax.broadcasted_iota(jnp.int32, (reach, reach), 1)
    tap_column = jnp.sum(jnp.where(at_sub == at_lane, taps[...], 0.0), axis=1, keepdims=True)

    def band(shift):
        at_sub = lax.broadcasted_iota(jnp.int32, (reach, WIDE), 0)
        at_lane = lax.broadcasted_iota(jnp.int32, (reach, WIDE), 1)
        origin = jnp.sum(
            jnp.where(at_lane == (at_sub + 1 - shift + WIDE) % WIDE, tap_column, 0.0),
            axis=0,
            keepdims=True,
        )
        origin = jnp.broadcast_to(origin, (PATCH, WIDE))
        return pltpu.roll(origin, 0, 1, stride=1, stride_axis=0)

    across = band(0)
    lane = lax.broadcasted_iota(jnp.int32, (PATCH, LANES), 1)
    edges = jnp.where(
        lane < HALO,
        across[:, 0:LANES],
        jnp.where(lane < 2 * HALO, across[:, PATCH:], 0.0),
    )
    along = jnp.concatenate([band(HALO)[:, 0:PATCH], edges], axis=1)

    for n, (dp, dc, _, _) in enumerate(moves):

        @pl.when(inside(dp, dc))
        def _():
            halo_copy(n).wait_send()

        @pl.when(inside(-dp, -dc))
        def _():
            halo_copy(n).wait_recv()

    turned = halo[...].T
    image[HALO : HALO + PATCH, PATCH:] = turned[0:PATCH, :]
    image[0:HALO, PATCH:] = turned[PATCH + LANES - HALO : PATCH + LANES, :]
    image[PATCH + HALO : PATCH + 2 * HALO, PATCH:] = turned[PATCH + LANES : PATCH + LANES + HALO, :]
    partial = split_dot(across, image[...], ((1,), (0,)))
    detection[...] = split_dot(along, partial, ((1,), (1,)))


def finish(coadd, detection, coadd_out, detection_out, sems):
    first = pltpu.make_async_copy(coadd, coadd_out, sems.at[0])
    second = pltpu.make_async_copy(detection, detection_out, sems.at[1])
    first.start()
    second.start()
    first.wait()
    second.wait()


def shards(
    blocks,
    owner,
    row_offset,
    col_offset,
    exposure,
    basis_rows,
    basis_cols,
    coef_table,
    weight_table,
    det_taps,
):
    nrow = lax.axis_size("prow")
    ncol = lax.axis_size("pcol")
    owners = nrow * ncol
    count, rows, cols = blocks.shape
    kinds, taps = basis_rows.shape
    slots = owners * CAP
    vmem = pl.BlockSpec(memory_space=pltpu.VMEM)

    tract = jax.ShapeDtypeStruct((PATCH, PATCH), jnp.float32)
    even = kinds + kinds % 2
    coadd, detection = pl.pallas_call(
        functools.partial(whole_kernel, nrow, ncol),
        out_shape=(pltpu.VMEM((PATCH, PATCH), jnp.float32),) * 2,
        in_specs=[vmem] * 9 + [pl.BlockSpec(memory_space=pl.ANY)],
        out_specs=(vmem, vmem),
        scratch_shapes=[
            pltpu.VMEM((count, rows, cols), jnp.bfloat16),
            pltpu.VMEM((1, slots), jnp.int32),
            pltpu.SMEM((1, slots), jnp.int32),
            pltpu.VMEM((nrow, ncol, 1, LANES), jnp.int32),
            pltpu.VMEM((slots, kinds * cols), jnp.float32),
            pltpu.VMEM((cols, kinds * cols), jnp.bfloat16),
            pltpu.VMEM((rows, even * rows), jnp.bfloat16),
            pltpu.VMEM((kinds * rows, MGROUP * CAP * cols), jnp.bfloat16),
            pltpu.VMEM((owners, CAP * rows, cols), jnp.bfloat16),
            pltpu.VMEM((owners, CAP * rows, cols), jnp.bfloat16),
            pltpu.VMEM((ncol, nrow, 1, LANES), jnp.int32),
            pltpu.VMEM((ncol, nrow, 1, LANES), jnp.int32),
            pltpu.VMEM((PATCH, PATCH), jnp.float32),
            pltpu.VMEM((WIDE, WIDE), jnp.float32),
            pltpu.VMEM((LANES, PATCH + 2 * LANES), jnp.float32),
            pltpu.SemaphoreType.DMA((4,)),
            pltpu.SemaphoreType.DMA((2, owners)),
            pltpu.SemaphoreType.DMA((2, 8)),
            pltpu.SemaphoreType.DMA((2, nrow)),
            pltpu.SemaphoreType.DMA((2, ncol)),
        ],
        compiler_params=pltpu.CompilerParams(
            collective_id=0, has_side_effects=True, vmem_limit_bytes=56 * 1024 * 1024
        ),
        name="whole",
    )(
        owner.reshape(1, count),
        exposure[None],
        row_offset[None],
        col_offset[None],
        weight_table[None],
        coef_table.T,
        basis_rows,
        basis_cols,
        det_taps[None],
        blocks,
    )
    return pl.pallas_call(
        finish,
        out_shape=(tract, tract),
        in_specs=[vmem] * 2,
        out_specs=(pl.BlockSpec(memory_space=pl.ANY),) * 2,
        scratch_shapes=[pltpu.SemaphoreType.DMA((2,))],
        compiler_params=pltpu.CompilerParams(vmem_limit_bytes=2 * 1024 * 1024),
        name="finish",
    )(coadd, detection)


def solution(mesh):
    in_specs = (
        P(("prow", "pcol"), None, None),
        P(("prow", "pcol"), None),
        P(("prow", "pcol")),
        P(("prow", "pcol")),
        P(("prow", "pcol")),
        P(),
        P(),
        P(),
        P(),
        P(),
    )
    out_specs = (P("prow", "pcol"), P("prow", "pcol"))
    return jax.shard_map(shards, mesh=mesh, in_specs=in_specs, out_specs=out_specs, check_vma=False)
```

```python
import functools

import jax
import jax.numpy as jnp
from jax import lax
from jax.experimental import pallas as pl
from jax.experimental.pallas import tpu as pltpu
from jax.sharding import PartitionSpec as P

DET_R = 15
PATCH = 384
CAP = 2
LANES = 128
MESH = pl.DeviceIdType.MESH
EXACT = lax.Precision.HIGHEST


HALO = 16
MGROUP = 4
GROUP = 8
PIECES = 4
WIDE = 512


def split_dot(left, right, dims):
    def parts(value):
        high = value.astype(jnp.bfloat16)
        return high, (value - high.astype(jnp.float32)).astype(jnp.bfloat16)

    (a, b), (c, d) = parts(left), parts(right)
    dot = functools.partial(
        lax.dot_general, dimension_numbers=(dims, ((), ())), preferred_element_type=jnp.float32
    )
    return dot(a, c) + (dot(a, d) + dot(b, c))


def prepare(kinds, owner, exposure, row_offset, col_offset, weights, coef_table, picks_out, told_out, coef_out):
    count = owner.shape[1]
    entries = weights.shape[1]
    slots = coef_out.shape[0]
    owners = slots // CAP
    at_sub = lax.broadcasted_iota(jnp.int32, (count, count), 0)
    at_lane = lax.broadcasted_iota(jnp.int32, (count, count), 1)

    def column(row):
        spread = jnp.broadcast_to(row, (count, count))
        return jnp.sum(jnp.where(at_sub == at_lane, spread, 0), axis=1, keepdims=True)

    same = jnp.where((column(owner[...]) == owner[...]) & (at_sub < at_lane), 1, 0)
    slot = owner[...] * CAP + jnp.sum(same, axis=0, keepdims=True)
    at_slot = lax.broadcasted_iota(jnp.int32, (count, slots), 1) == column(slot)
    numbers = lax.broadcasted_iota(jnp.int32, (count, slots), 0)
    picks_out[...] = jnp.sum(jnp.where(at_slot, numbers, 0), axis=0, keepdims=True)
    lane = lax.broadcasted_iota(jnp.int32, (owners, LANES), 1)
    told = jnp.zeros((owners, LANES), jnp.int32)
    for j in range(CAP):
        own = lax.broadcasted_iota(jnp.int32, (owners, count), 0) * CAP + j == slot
        values = (jnp.ones_like(slot), exposure[...], row_offset[...], col_offset[...])
        for n, value in enumerate(values):
            found = jnp.sum(jnp.where(own, value, 0), axis=1, keepdims=True)
            told = jnp.where(lane == 4 * j + n, found, told)
    for o in range(owners):
        mate = (o + owners // 2) % owners
        told_out[o, 0:1, :] = told[o : o + 1, :]
        told_out[o, 1:2, :] = told[mate : mate + 1, :]
    own = lax.broadcasted_iota(jnp.int32, (slots, count), 0) == slot
    index = jnp.sum(jnp.where(own, exposure[...], 0), axis=1, keepdims=True)
    hits = lax.broadcasted_iota(jnp.int32, (slots, entries), 1) == index
    weight = jnp.sum(jnp.where(hits, weights[...], 0.0), axis=1, keepdims=True)
    weight = weight.astype(jnp.bfloat16).astype(jnp.float32)
    cols = coef_out.shape[1] // kinds
    coefs = lax.dot_general(
        hits.astype(jnp.float32),
        coef_table[...],
        (((1,), (1,)), ((), ())),
        precision=EXACT,
        preferred_element_type=jnp.float32,
    )
    coefs = coefs * weight
    for k in range(kinds):
        coef_out[:, k * cols : (k + 1) * cols] = jnp.broadcast_to(
            coefs[:, k : k + 1], (slots, cols)
        )


def build_tables(basis_rows, basis_cols, col_out, row_out):
    kinds, taps = basis_rows.shape
    half = taps // 2
    rows, cols = row_out.shape[0], col_out.shape[0]
    tap = lax.broadcasted_iota(jnp.int32, (taps, LANES), 0)
    lane = lax.broadcasted_iota(jnp.int32, (taps, LANES), 1)

    def spread(value, target):
        hot = jnp.where(lane == (target + LANES) % LANES, 1.0, 0.0).astype(jnp.bfloat16)
        return jnp.dot(value[...], hot, preferred_element_type=jnp.float32)

    col_src = spread(basis_cols, half - tap)
    even = spread(basis_rows, tap - half)
    odd = spread(basis_rows, tap - half + rows)
    near = jnp.abs(
        lax.broadcasted_iota(jnp.int32, (cols, LANES), 1)
        - lax.broadcasted_iota(jnp.int32, (cols, LANES), 0)
    )
    for k in range(kinds):
        source = jnp.broadcast_to(col_src[k : k + 1, :], (cols, LANES))
        rolled = pltpu.roll(source, 0, 1, stride=1, stride_axis=0)
        col_out[:, k * LANES : (k + 1) * LANES] = jnp.where(near <= half, rolled, 0.0).astype(
            jnp.bfloat16
        )
    near = jnp.abs(
        lax.broadcasted_iota(jnp.int32, (rows, LANES), 1) % rows
        - lax.broadcasted_iota(jnp.int32, (rows, LANES), 0)
    )
    for k in range(0, kinds, 2):
        source = even[k : k + 1, :]
        if k + 1 < kinds:
            source = source + odd[k + 1 : k + 2, :]
        rolled = pltpu.roll(
            jnp.broadcast_to(source, (rows, LANES)), 0, 1, stride=1, stride_axis=0
        )
        row_out[:, k * rows : k * rows + LANES] = jnp.where(near <= half, rolled, 0.0).astype(
            jnp.bfloat16
        )


def whole_kernel(
    nrow,
    ncol,
    small_sources,
    source_blocks,
    coadd,
    detection,
    small,
    blocks,
    pick_row,
    picks,
    info,
    coefs,
    col_table,
    row_table,
    sections,
    outgoing,
    arrived,
    passing,
    shifted_rows,
    shifted_to,
    sums_out,
    sums_in,
    heard,
    total,
    image,
    halo,
    sems,
    data_sems,
    halo_sems,
    pass_sems,
    sum_sems,
    load_sems,
):
    owner, exposure, row_offset, col_offset, weights, coef_table, basis_rows, basis_cols, taps = small
    owners = nrow * ncol
    prow, pcol = lax.axis_index("prow"), lax.axis_index("pcol")
    me = prow * ncol + pcol
    rows, cols = blocks.shape[1:]
    kinds = basis_rows.shape[0]
    span = nrow // 2
    half = span // 2
    each = half * ncol
    side, level = prow // span, prow % span
    inner = (level // half + side) % 2
    mate = (prow + span) % nrow
    local = level * ncol + pcol

    def turn(i):
        phase, j = i // each, i % each
        col = (pcol + 1 + i) % ncol
        across = (level + 1 + j // ncol) % half
        passed = phase == inner
        direct = phase == 1 - inner
        at = jnp.where(passed, (1 - side) * half + across, side * half + across)
        at = jnp.where(phase < 2, at, (level + 1 + (i - 2 * each) // ncol) % span)
        patch = (jnp.where(phase < 2, 1 - side, side) * span + at) * ncol + col
        dest = (jnp.where(direct, 1 - side, side) * span + at) * ncol + col
        return patch, dest, passed

    def far_source(i):
        at = (side * half + i // ncol) % span
        return ((1 - side) * span + at) * ncol + (pcol + 2 * ncol - 1 - i % ncol) % ncol

    def near_source(i):
        at = (level + 2 * span - 1 - i // ncol) % span
        return (side * span + at) * ncol + (pcol + 2 * ncol - 1 - i % ncol) % ncol

    def place(device):
        return (device // ncol, device % ncol)

    barrier = pltpu.get_barrier_semaphore()
    loads = [
        pltpu.make_async_copy(source, target, load_sems.at[n])
        for n, (source, target) in enumerate(zip(small_sources, small))
    ]
    for load in loads:
        load.start()
    load_blocks = pltpu.make_async_copy(source_blocks, blocks, sems.at[3])
    load_blocks.start()

    def greet(i, carry):
        other = lax.rem(me + i, owners)
        pl.semaphore_signal(barrier, inc=1, device_id=place(other), device_id_type=MESH)
        return carry

    lax.fori_loop(1, owners, greet, 0)
    halo[...] = jnp.zeros_like(halo)
    image[0:HALO, :] = jnp.zeros((HALO, WIDE), jnp.float32)
    image[PATCH + HALO :, :] = jnp.zeros((WIDE - PATCH - HALO, WIDE), jnp.float32)
    total[...] = jnp.zeros_like(total)
    for load in loads:
        load.wait()
    prepare(
        kinds, owner, exposure, row_offset, col_offset, weights, coef_table, pick_row, info, coefs
    )
    lift = pltpu.make_async_copy(pick_row, picks, sems.at[2])
    lift.start()
    build_tables(basis_rows, basis_cols, col_table, row_table)
    lift.wait()
    load_blocks.wait()

    def tell(i, carry):
        other = lax.rem(me + i, owners)
        pltpu.make_async_remote_copy(
            src_ref=info.at[other],
            dst_ref=heard.at[me],
            send_sem=sems.at[0],
            recv_sem=sems.at[1],
            device_id=place(other),
            device_id_type=MESH,
        ).start()
        return carry

    others = pl.ds(0, owners - 1)

    mgroup = MGROUP

    def matched_group(first):
        slots_of = [
            turn(first + n)[0] * CAP + j for n in range(mgroup) for j in range(CAP)
        ]
        pixels = jnp.concatenate([blocks[picks[0, s]] for s in slots_of], axis=0)
        coefs_of = [coefs[pl.ds(s, 1), :] for s in slots_of]
        section = jnp.dot(pixels, col_table[...], preferred_element_type=jnp.float32)
        for k in range(kinds):
            for n, coef in enumerate(coefs_of):
                part = section[n * rows : (n + 1) * rows, k * cols : (k + 1) * cols]
                sections[k * rows : (k + 1) * rows, n * cols : (n + 1) * cols] = (
                    coef[:, k * cols : (k + 1) * cols] * part
                ).astype(jnp.bfloat16)
        matched = jnp.dot(
            row_table[:, 0 : kinds * rows], sections[...], preferred_element_type=jnp.float32
        ).astype(jnp.bfloat16)
        for n in range(mgroup):
            for j in range(CAP):
                m = n * CAP + j
                outgoing[turn(first + n)[0], j * rows : (j + 1) * rows, :] = matched[
                    :, m * cols : (m + 1) * cols
                ]

    def data_copy(patch, dest, origin):
        return pltpu.make_async_remote_copy(
            src_ref=outgoing.at[patch],
            dst_ref=arrived.at[origin],
            send_sem=data_sems.at[0, patch],
            recv_sem=data_sems.at[1, origin],
            device_id=place(dest),
            device_id_type=MESH,
        )

    def pass_copy(patch, dest, origin):
        return pltpu.make_async_remote_copy(
            src_ref=outgoing.at[patch],
            dst_ref=passing.at[origin],
            send_sem=data_sems.at[0, patch],
            recv_sem=pass_sems.at[origin],
            device_id=place(dest),
            device_id_type=MESH,
        )

    pieces = sum_sems.shape[1]
    deep = PATCH // pieces

    def sum_copy(n):
        piece = pl.ds(n * deep, deep)
        return pltpu.make_async_remote_copy(
            src_ref=sums_out.at[piece],
            dst_ref=sums_in.at[piece],
            send_sem=sum_sems.at[0, n],
            recv_sem=sum_sems.at[1, n],
            device_id=(mate, pcol),
            device_id_type=MESH,
        )

    offset = lax.broadcasted_iota(jnp.int32, (cols, PATCH), 1) - lax.broadcasted_iota(
        jnp.int32, (cols, PATCH), 0
    )
    group = GROUP
    many = group * CAP

    def shift_group(origins, which, buffer, slots_at):
        lane = lax.broadcasted_iota(jnp.int32, (1, many * rows), 1)
        target = lane % rows
        shifted = []
        for n, origin in enumerate(origins):
            letter = heard[origin, which : which + 1, :]
            for j in range(CAP):
                live, _, top, left = (letter[:, 4 * j + m : 4 * j + m + 1] for m in range(4))
                left = jnp.where(live > 0, left, -PATCH)
                hot = jnp.where(offset == left, 1.0, 0.0).astype(jnp.bfloat16)
                block = buffer[slots_at[n], j * rows : (j + 1) * rows, :]
                shifted.append(
                    jnp.dot(block, hot, preferred_element_type=jnp.float32).astype(jnp.bfloat16)
                )
                target = target + jnp.where(lane // rows == n * CAP + j, top, 0)
        return jnp.concatenate(shifted, axis=0), target

    def pass_shift(g, carry):
        slots_at, origins = [], []
        for n in range(group):
            i = g * group + n
            origin = near_source(i)
            slot = origin % (span * ncol)

            @pl.when(i < span * ncol - 1)
            def _():
                pass_copy(origin, origin, slot).wait_recv()

            slots_at.append(slot)
            origins.append(origin)
        shifted, target = shift_group(origins, 1, passing, slots_at)
        shifted_rows[pl.ds(g * many * rows, many * rows), :] = shifted
        shifted_to[g] = target
        return carry

    def send_sum(n, carry):
        down = lax.broadcasted_iota(jnp.int32, (deep, many * rows), 0) + n * deep
        hot = jnp.concatenate(
            [
                jnp.where(down == shifted_to[g], 1.0, 0.0).astype(jnp.bfloat16)
                for g in range(span * ncol // group)
            ],
            axis=1,
        )
        sums_out[pl.ds(n * deep, deep), :] = jnp.dot(
            hot, shifted_rows[...], preferred_element_type=jnp.float32
        ).astype(jnp.bfloat16)
        sum_copy(n).start()
        return carry

    def send(g, carry):
        matched_group(g * mgroup)

        @pl.when(g == 0)
        def _():
            pl.semaphore_wait(barrier, owners - 1)
            lax.fori_loop(1, owners, tell, 0)
            heard[me] = info[me]

        def start(i, carry):
            patch, dest, passed = turn(i)

            @pl.when((dest != me) & passed)
            def _():
                pass_copy(patch, dest, local).start()

            @pl.when((dest != me) & jnp.logical_not(passed))
            def _():
                data_copy(patch, dest, me).start()

            @pl.when((dest == me) & passed)
            def _():
                passing[local] = outgoing[patch]

            return carry

        last_held = 2 * each // mgroup - 1
        held = (inner == 0) & (g >= each // mgroup) & (g <= last_held)

        @pl.when(jnp.logical_not(held))
        def _():
            lax.fori_loop(g * mgroup, (g + 1) * mgroup, start, 0)

        @pl.when(held & (g == last_held))
        def _():
            def gone(i, carry):
                patch, dest, _ = turn(i)
                pass_copy(patch, dest, local).wait_send()
                return carry

            lax.fori_loop(0, each, gone, 0)
            lax.fori_loop(each, 2 * each, start, 0)

        return carry

    lax.fori_loop(0, owners // mgroup, send, 0)
    arrived[me] = outgoing[me]
    pltpu.make_async_copy(heard.at[others], heard.at[others], sems.at[1]).wait()

    @pl.when(inner == 1)
    def _():
        lax.fori_loop(0, span * ncol // group, pass_shift, 0)
        lax.fori_loop(0, pieces, send_sum, 0)


    wide = lax.broadcasted_iota(jnp.int32, (owners, PATCH), 1)
    entries = weights.shape[1]
    letters = jnp.concatenate([heard[o, 0:1, :] for o in range(owners)], axis=0)
    depth = jnp.zeros((PATCH, PATCH), jnp.float32)
    for j in range(CAP):
        live, entry, top, left = (letters[:, 4 * j + n : 4 * j + n + 1] for n in range(4))
        hits = lax.broadcasted_iota(jnp.int32, (owners, entries), 1) == entry
        weight = jnp.sum(jnp.where(hits, weights[...], 0.0), axis=1, keepdims=True)
        weight = jnp.where(live > 0, weight, 0.0)
        row_weight = jnp.where((wide >= top) & (wide < top + rows), weight, 0.0)
        col_cover = jnp.where((wide >= left) & (wide < left + cols), 1.0, 0.0)
        depth = depth + lax.dot_general(
            row_weight.astype(jnp.bfloat16),
            col_cover.astype(jnp.bfloat16),
            (((0,), (0,)), ((), ())),
            preferred_element_type=jnp.float32,
        )
    coadd[...] = jnp.maximum(depth, 1.0)

    down = lax.broadcasted_iota(jnp.int32, (PATCH, many * rows), 0)

    def gather(source, limit):
        def step(g, carry):
            origins = [source(g * group + n) for n in range(group)]
            for n, origin in enumerate(origins):

                @pl.when(g * group + n < limit)
                def _():
                    data_copy(origin, origin, origin).wait_recv()

            shifted, target = shift_group(origins, 0, arrived, origins)
            hot = jnp.where(down == target, 1.0, 0.0).astype(jnp.bfloat16)
            total[...] += jnp.dot(hot, shifted, preferred_element_type=jnp.float32)
            return carry

        lax.fori_loop(0, span * ncol // group, step, 0)

    @pl.when(inner == 1)
    def _():
        gather(far_source, span * ncol)

    gather(near_source, span * ncol - 1)

    @pl.when(inner == 0)
    def _():
        for n in range(pieces):
            sum_copy(n).wait_recv()
        total[...] += sums_in[...].astype(jnp.float32)

    coadd[...] = total[...] / coadd[...]

    first_rows, last_rows = pl.ds(0, HALO), pl.ds(PATCH - HALO, HALO)
    first, last, whole = pl.ds(0, LANES), pl.ds(PATCH - LANES, LANES), pl.ds(0, PATCH)
    left_tile, right_tile = pl.ds(PATCH, LANES), pl.ds(PATCH + LANES, LANES)
    below = pl.ds(HALO, HALO)
    moves = (
        (1, 0, coadd.at[last_rows, whole], halo.at[first_rows, whole]),
        (-1, 0, coadd.at[first_rows, whole], halo.at[below, whole]),
        (1, 1, coadd.at[last_rows, last], halo.at[first_rows, left_tile]),
        (1, -1, coadd.at[last_rows, first], halo.at[first_rows, right_tile]),
        (-1, 1, coadd.at[first_rows, last], halo.at[below, left_tile]),
        (-1, -1, coadd.at[first_rows, first], halo.at[below, right_tile]),
        (0, -1, image.at[below, whole], image.at[pl.ds(PATCH + HALO, HALO), whole]),
        (0, 1, image.at[pl.ds(PATCH, HALO), whole], image.at[first_rows, whole]),
    )

    def inside(dp, dc):
        row, col = prow + dp, pcol + dc
        return (row >= 0) & (row < nrow) & (col >= 0) & (col < ncol)

    def halo_copy(n):
        dp, dc, origin, target = moves[n]
        return pltpu.make_async_remote_copy(
            src_ref=origin,
            dst_ref=target,
            send_sem=halo_sems.at[0, n],
            recv_sem=halo_sems.at[1, n],
            device_id=(prow + dp, pcol + dc),
            device_id_type=MESH,
        )

    for n, (dp, dc, _, _) in enumerate(moves):
        if dp == 0 and dc < 0:
            image[HALO : HALO + PATCH, 0:PATCH] = coadd[...].T

        @pl.when(inside(dp, dc))
        def _():
            halo_copy(n).start()

    def sent(i, carry):
        patch, dest, passed = turn(i)
        gone = passed & (inner == 0)

        @pl.when((dest != me) & jnp.logical_not(gone))
        def _():
            data_copy(patch, dest, me).wait_send()

        return carry

    lax.fori_loop(0, owners, sent, 0)

    @pl.when(inner == 1)
    def _():
        for n in range(pieces):
            sum_copy(n).wait_send()

    pltpu.make_async_copy(info.at[others], info.at[others], sems.at[0]).wait()

    reach = taps.shape[1]
    at_sub = lax.broadcasted_iota(jnp.int32, (reach, reach), 0)
    at_lane = lax.broadcasted_iota(jnp.int32, (reach, reach), 1)
    tap_column = jnp.sum(jnp.where(at_sub == at_lane, taps[...], 0.0), axis=1, keepdims=True)

    def band(shift):
        at_sub = lax.broadcasted_iota(jnp.int32, (reach, WIDE), 0)
        at_lane = lax.broadcasted_iota(jnp.int32, (reach, WIDE), 1)
        origin = jnp.sum(
            jnp.where(at_lane == (at_sub + 1 - shift + WIDE) % WIDE, tap_column, 0.0),
            axis=0,
            keepdims=True,
        )
        origin = jnp.broadcast_to(origin, (PATCH, WIDE))
        return pltpu.roll(origin, 0, 1, stride=1, stride_axis=0)

    across = band(0)
    lane = lax.broadcasted_iota(jnp.int32, (PATCH, LANES), 1)
    edges = jnp.where(
        lane < HALO,
        across[:, 0:LANES],
        jnp.where(lane < 2 * HALO, across[:, PATCH:], 0.0),
    )
    along = jnp.concatenate([band(HALO)[:, 0:PATCH], edges], axis=1)

    for n, (dp, dc, _, _) in enumerate(moves):

        @pl.when(inside(dp, dc))
        def _():
            halo_copy(n).wait_send()

        @pl.when(inside(-dp, -dc))
        def _():
            halo_copy(n).wait_recv()

    turned = halo[...].T
    image[HALO : HALO + PATCH, PATCH:] = turned[0:PATCH, :]
    image[0:HALO, PATCH:] = turned[PATCH + LANES - HALO : PATCH + LANES, :]
    image[PATCH + HALO : PATCH + 2 * HALO, PATCH:] = turned[PATCH + LANES : PATCH + LANES + HALO, :]
    partial = split_dot(across, image[...], ((1,), (0,)))
    detection[...] = split_dot(along, partial, ((1,), (1,)))


def finish(coadd, detection, coadd_out, detection_out, sems):
    first = pltpu.make_async_copy(coadd, coadd_out, sems.at[0])
    second = pltpu.make_async_copy(detection, detection_out, sems.at[1])
    first.start()
    second.start()
    first.wait()
    second.wait()


def shards(
    blocks,
    owner,
    row_offset,
    col_offset,
    exposure,
    basis_rows,
    basis_cols,
    coef_table,
    weight_table,
    det_taps,
):
    nrow = lax.axis_size("prow")
    ncol = lax.axis_size("pcol")
    owners = nrow * ncol
    count, rows, cols = blocks.shape
    kinds, taps = basis_rows.shape
    slots = owners * CAP
    span = nrow // 2
    vmem = pl.BlockSpec(memory_space=pltpu.VMEM)
    anywhere = pl.BlockSpec(memory_space=pl.ANY)
    small = (
        owner.reshape(1, count),
        exposure[None],
        row_offset[None],
        col_offset[None],
        weight_table[None],
        coef_table.T,
        basis_rows,
        basis_cols,
        det_taps[None],
    )

    tract = jax.ShapeDtypeStruct((PATCH, PATCH), jnp.float32)
    even = kinds + kinds % 2
    coadd, detection = pl.pallas_call(
        functools.partial(whole_kernel, nrow, ncol),
        out_shape=(pltpu.VMEM((PATCH, PATCH), jnp.float32),) * 2,
        in_specs=[tuple(anywhere for _ in small), anywhere],
        out_specs=(vmem, vmem),
        scratch_shapes=[
            tuple(pltpu.VMEM(x.shape, x.dtype) for x in small),
            pltpu.VMEM((count, rows, cols), jnp.bfloat16),
            pltpu.VMEM((1, slots), jnp.int32),
            pltpu.SMEM((1, slots), jnp.int32),
            pltpu.VMEM((owners, 2, LANES), jnp.int32),
            pltpu.VMEM((slots, kinds * cols), jnp.float32),
            pltpu.VMEM((cols, kinds * cols), jnp.bfloat16),
            pltpu.VMEM((rows, even * rows), jnp.bfloat16),
            pltpu.VMEM((kinds * rows, MGROUP * CAP * cols), jnp.bfloat16),
            pltpu.VMEM((owners, CAP * rows, cols), jnp.bfloat16),
            pltpu.VMEM((owners, CAP * rows, cols), jnp.bfloat16),
            pltpu.VMEM((span * ncol, CAP * rows, cols), jnp.bfloat16),
            pltpu.VMEM((span * ncol * CAP * rows, PATCH), jnp.bfloat16),
            pltpu.VMEM((span * ncol // GROUP, 1, GROUP * CAP * rows), jnp.int32),
            pltpu.VMEM((PATCH, PATCH), jnp.bfloat16),
            pltpu.VMEM((PATCH, PATCH), jnp.bfloat16),
            pltpu.VMEM((owners, 2, LANES), jnp.int32),
            pltpu.VMEM((PATCH, PATCH), jnp.float32),
            pltpu.VMEM((WIDE, WIDE), jnp.float32),
            pltpu.VMEM((LANES, PATCH + 2 * LANES), jnp.float32),
            pltpu.SemaphoreType.DMA((4,)),
            pltpu.SemaphoreType.DMA((2, owners)),
            pltpu.SemaphoreType.DMA((2, 8)),
            pltpu.SemaphoreType.DMA((span * ncol,)),
            pltpu.SemaphoreType.DMA((2, PIECES)),
            pltpu.SemaphoreType.DMA((len(small),)),
        ],
        compiler_params=pltpu.CompilerParams(
            collective_id=0, has_side_effects=True, vmem_limit_bytes=56 * 1024 * 1024
        ),
        name="whole",
    )(small, blocks)
    return pl.pallas_call(
        finish,
        out_shape=(tract, tract),
        in_specs=[vmem] * 2,
        out_specs=(pl.BlockSpec(memory_space=pl.ANY),) * 2,
        scratch_shapes=[pltpu.SemaphoreType.DMA((2,))],
        compiler_params=pltpu.CompilerParams(vmem_limit_bytes=2 * 1024 * 1024),
        name="finish",
    )(coadd, detection)


def solution(mesh):
    in_specs = (
        P(("prow", "pcol"), None, None),
        P(("prow", "pcol"), None),
        P(("prow", "pcol")),
        P(("prow", "pcol")),
        P(("prow", "pcol")),
        P(),
        P(),
        P(),
        P(),
        P(),
    )
    out_specs = (P("prow", "pcol"), P("prow", "pcol"))
    return jax.shard_map(shards, mesh=mesh, in_specs=in_specs, out_specs=out_specs, check_vma=False)
```

```python
import functools

import jax
import jax.numpy as jnp
from jax import lax
from jax.experimental import pallas as pl
from jax.experimental.pallas import tpu as pltpu
from jax.sharding import PartitionSpec as P

DET_R = 15
PATCH = 384
CAP = 2
LANES = 128
MESH = pl.DeviceIdType.MESH
EXACT = lax.Precision.HIGHEST


HALO = 16
MGROUP = 4
GROUP = 8
PIECES = 4
WIDE = 512


def half_dot(left, right, dims):
    return lax.dot_general(
        left.astype(jnp.bfloat16),
        right.astype(jnp.bfloat16),
        (dims, ((), ())),
        preferred_element_type=jnp.float32,
    )


def prepare(kinds, owner, exposure, row_offset, col_offset, weights, coef_table, picks_out, told_out, coef_out):
    count = owner.shape[1]
    entries = weights.shape[1]
    slots = coef_out.shape[0]
    owners = slots // CAP
    at_sub = lax.broadcasted_iota(jnp.int32, (count, count), 0)
    at_lane = lax.broadcasted_iota(jnp.int32, (count, count), 1)

    def column(row):
        spread = jnp.broadcast_to(row, (count, count))
        return jnp.sum(jnp.where(at_sub == at_lane, spread, 0), axis=1, keepdims=True)

    same = jnp.where((column(owner[...]) == owner[...]) & (at_sub < at_lane), 1, 0)
    slot = owner[...] * CAP + jnp.sum(same, axis=0, keepdims=True)
    at_slot = lax.broadcasted_iota(jnp.int32, (count, slots), 1) == column(slot)
    numbers = lax.broadcasted_iota(jnp.int32, (count, slots), 0)
    picks_out[...] = jnp.sum(jnp.where(at_slot, numbers, 0), axis=0, keepdims=True)
    lane = lax.broadcasted_iota(jnp.int32, (owners, LANES), 1)
    told = jnp.zeros((owners, LANES), jnp.int32)
    for j in range(CAP):
        own = lax.broadcasted_iota(jnp.int32, (owners, count), 0) * CAP + j == slot
        values = (jnp.ones_like(slot), exposure[...], row_offset[...], col_offset[...])
        for n, value in enumerate(values):
            found = jnp.sum(jnp.where(own, value, 0), axis=1, keepdims=True)
            told = jnp.where(lane == 4 * j + n, found, told)
    for o in range(owners):
        mate = (o + owners // 2) % owners
        told_out[o, 0:1, :] = told[o : o + 1, :]
        told_out[o, 1:2, :] = told[mate : mate + 1, :]
    own = lax.broadcasted_iota(jnp.int32, (slots, count), 0) == slot
    index = jnp.sum(jnp.where(own, exposure[...], 0), axis=1, keepdims=True)
    hits = lax.broadcasted_iota(jnp.int32, (slots, entries), 1) == index
    weight = jnp.sum(jnp.where(hits, weights[...], 0.0), axis=1, keepdims=True)
    weight = weight.astype(jnp.bfloat16).astype(jnp.float32)
    cols = coef_out.shape[1] // kinds
    coefs = lax.dot_general(
        hits.astype(jnp.float32),
        coef_table[...],
        (((1,), (1,)), ((), ())),
        precision=EXACT,
        preferred_element_type=jnp.float32,
    )
    coefs = coefs * weight
    for k in range(kinds):
        coef_out[:, k * cols : (k + 1) * cols] = jnp.broadcast_to(
            coefs[:, k : k + 1], (slots, cols)
        )


def build_tables(basis_rows, basis_cols, col_out, row_out):
    kinds, taps = basis_rows.shape
    half = taps // 2
    rows, cols = row_out.shape[0], col_out.shape[0]
    tap = lax.broadcasted_iota(jnp.int32, (taps, LANES), 0)
    lane = lax.broadcasted_iota(jnp.int32, (taps, LANES), 1)

    def spread(value, target):
        hot = jnp.where(lane == (target + LANES) % LANES, 1.0, 0.0).astype(jnp.bfloat16)
        return jnp.dot(value[...], hot, preferred_element_type=jnp.float32)

    col_src = spread(basis_cols, half - tap)
    even = spread(basis_rows, tap - half)
    odd = spread(basis_rows, tap - half + rows)
    near = jnp.abs(
        lax.broadcasted_iota(jnp.int32, (cols, LANES), 1)
        - lax.broadcasted_iota(jnp.int32, (cols, LANES), 0)
    )
    for k in range(kinds):
        source = jnp.broadcast_to(col_src[k : k + 1, :], (cols, LANES))
        rolled = pltpu.roll(source, 0, 1, stride=1, stride_axis=0)
        col_out[:, k * LANES : (k + 1) * LANES] = jnp.where(near <= half, rolled, 0.0).astype(
            jnp.bfloat16
        )
    near = jnp.abs(
        lax.broadcasted_iota(jnp.int32, (rows, LANES), 1) % rows
        - lax.broadcasted_iota(jnp.int32, (rows, LANES), 0)
    )
    for k in range(0, kinds, 2):
        source = even[k : k + 1, :]
        if k + 1 < kinds:
            source = source + odd[k + 1 : k + 2, :]
        rolled = pltpu.roll(
            jnp.broadcast_to(source, (rows, LANES)), 0, 1, stride=1, stride_axis=0
        )
        row_out[:, k * rows : k * rows + LANES] = jnp.where(near <= half, rolled, 0.0).astype(
            jnp.bfloat16
        )


def whole_kernel(
    nrow,
    ncol,
    small_sources,
    source_blocks,
    coadd,
    detection,
    small,
    blocks,
    pick_row,
    picks,
    info,
    coefs,
    col_table,
    row_table,
    sections,
    outgoing,
    arrived,
    passing,
    shifted_rows,
    shifted_to,
    sums_out,
    sums_in,
    heard,
    total,
    image,
    halo,
    sems,
    data_sems,
    halo_sems,
    pass_sems,
    sum_sems,
    load_sems,
):
    owner, exposure, row_offset, col_offset, weights, coef_table, basis_rows, basis_cols, taps = small
    owners = nrow * ncol
    prow, pcol = lax.axis_index("prow"), lax.axis_index("pcol")
    me = prow * ncol + pcol
    rows, cols = blocks.shape[1:]
    kinds = basis_rows.shape[0]
    span = nrow // 2
    half = span // 2
    each = half * ncol
    side, level = prow // span, prow % span
    inner = (level // half + side) % 2
    mate = (prow + span) % nrow
    local = level * ncol + pcol

    def turn(i):
        phase, j = i // each, i % each
        col = (pcol + 1 + i) % ncol
        across = (level + 1 + j // ncol) % half
        passed = phase == inner
        direct = phase == 1 - inner
        at = jnp.where(passed, (1 - side) * half + across, side * half + across)
        at = jnp.where(phase < 2, at, (level + 1 + (i - 2 * each) // ncol) % span)
        patch = (jnp.where(phase < 2, 1 - side, side) * span + at) * ncol + col
        dest = (jnp.where(direct, 1 - side, side) * span + at) * ncol + col
        return patch, dest, passed

    def far_source(i):
        at = (side * half + i // ncol) % span
        return ((1 - side) * span + at) * ncol + (pcol + 2 * ncol - 1 - i % ncol) % ncol

    def near_source(i):
        at = (level + 2 * span - 1 - i // ncol) % span
        return (side * span + at) * ncol + (pcol + 2 * ncol - 1 - i % ncol) % ncol

    def place(device):
        return (device // ncol, device % ncol)

    barrier = pltpu.get_barrier_semaphore()
    loads = [
        pltpu.make_async_copy(source, target, load_sems.at[n])
        for n, (source, target) in enumerate(zip(small_sources, small))
    ]
    for load in loads:
        load.start()
    load_blocks = pltpu.make_async_copy(source_blocks, blocks, sems.at[3])
    load_blocks.start()

    def greet(i, carry):
        other = lax.rem(me + i, owners)
        pl.semaphore_signal(barrier, inc=1, device_id=place(other), device_id_type=MESH)
        return carry

    lax.fori_loop(1, owners, greet, 0)
    halo[...] = jnp.zeros_like(halo)
    image[0:HALO, :] = jnp.zeros((HALO, WIDE), jnp.float32)
    image[PATCH + HALO :, :] = jnp.zeros((WIDE - PATCH - HALO, WIDE), jnp.float32)
    total[...] = jnp.zeros_like(total)
    for load in loads:
        load.wait()
    prepare(
        kinds, owner, exposure, row_offset, col_offset, weights, coef_table, pick_row, info, coefs
    )
    lift = pltpu.make_async_copy(pick_row, picks, sems.at[2])
    lift.start()
    build_tables(basis_rows, basis_cols, col_table, row_table)
    lift.wait()
    load_blocks.wait()

    def tell(i, carry):
        other = lax.rem(me + i, owners)
        pltpu.make_async_remote_copy(
            src_ref=info.at[other],
            dst_ref=heard.at[me],
            send_sem=sems.at[0],
            recv_sem=sems.at[1],
            device_id=place(other),
            device_id_type=MESH,
        ).start()
        return carry

    others = pl.ds(0, owners - 1)

    mgroup = MGROUP

    def matched_group(first):
        slots_of = [
            turn(first + n)[0] * CAP + j for n in range(mgroup) for j in range(CAP)
        ]
        pixels = jnp.concatenate([blocks[picks[0, s]] for s in slots_of], axis=0)
        coefs_of = [coefs[pl.ds(s, 1), :] for s in slots_of]
        section = jnp.dot(pixels, col_table[...], preferred_element_type=jnp.float32)
        for k in range(kinds):
            for n, coef in enumerate(coefs_of):
                part = section[n * rows : (n + 1) * rows, k * cols : (k + 1) * cols]
                sections[k * rows : (k + 1) * rows, n * cols : (n + 1) * cols] = (
                    coef[:, k * cols : (k + 1) * cols] * part
                ).astype(jnp.bfloat16)
        matched = jnp.dot(
            row_table[:, 0 : kinds * rows], sections[...], preferred_element_type=jnp.float32
        ).astype(jnp.bfloat16)
        for n in range(mgroup):
            for j in range(CAP):
                m = n * CAP + j
                outgoing[turn(first + n)[0], j * rows : (j + 1) * rows, :] = matched[
                    :, m * cols : (m + 1) * cols
                ]

    def data_copy(patch, dest, origin):
        return pltpu.make_async_remote_copy(
            src_ref=outgoing.at[patch],
            dst_ref=arrived.at[origin],
            send_sem=data_sems.at[0, patch],
            recv_sem=data_sems.at[1, origin],
            device_id=place(dest),
            device_id_type=MESH,
        )

    def pass_copy(patch, dest, origin):
        return pltpu.make_async_remote_copy(
            src_ref=outgoing.at[patch],
            dst_ref=passing.at[origin],
            send_sem=data_sems.at[0, patch],
            recv_sem=pass_sems.at[origin],
            device_id=place(dest),
            device_id_type=MESH,
        )

    pieces = sum_sems.shape[1]
    deep = PATCH // pieces

    def sum_copy(n):
        piece = pl.ds(n * deep, deep)
        return pltpu.make_async_remote_copy(
            src_ref=sums_out.at[piece],
            dst_ref=sums_in.at[piece],
            send_sem=sum_sems.at[0, n],
            recv_sem=sum_sems.at[1, n],
            device_id=(mate, pcol),
            device_id_type=MESH,
        )

    offset = lax.broadcasted_iota(jnp.int32, (cols, PATCH), 1) - lax.broadcasted_iota(
        jnp.int32, (cols, PATCH), 0
    )
    group = GROUP
    many = group * CAP

    def shift_group(origins, which, buffer, slots_at):
        lane = lax.broadcasted_iota(jnp.int32, (1, many * rows), 1)
        target = lane % rows
        shifted = []
        for n, origin in enumerate(origins):
            letter = heard[origin, which : which + 1, :]
            for j in range(CAP):
                live, _, top, left = (letter[:, 4 * j + m : 4 * j + m + 1] for m in range(4))
                left = jnp.where(live > 0, left, -PATCH)
                hot = jnp.where(offset == left, 1.0, 0.0).astype(jnp.bfloat16)
                block = buffer[slots_at[n], j * rows : (j + 1) * rows, :]
                shifted.append(
                    jnp.dot(block, hot, preferred_element_type=jnp.float32).astype(jnp.bfloat16)
                )
                target = target + jnp.where(lane // rows == n * CAP + j, top, 0)
        return jnp.concatenate(shifted, axis=0), target

    def pass_shift(g, carry):
        slots_at, origins = [], []
        for n in range(group):
            i = g * group + n
            origin = near_source(i)
            slot = origin % (span * ncol)

            @pl.when(i < span * ncol - 1)
            def _():
                pass_copy(origin, origin, slot).wait_recv()

            slots_at.append(slot)
            origins.append(origin)
        shifted, target = shift_group(origins, 1, passing, slots_at)
        shifted_rows[pl.ds(g * many * rows, many * rows), :] = shifted
        shifted_to[g] = target
        return carry

    def send_sum(n, carry):
        down = lax.broadcasted_iota(jnp.int32, (deep, many * rows), 0) + n * deep
        hot = jnp.concatenate(
            [
                jnp.where(down == shifted_to[g], 1.0, 0.0).astype(jnp.bfloat16)
                for g in range(span * ncol // group)
            ],
            axis=1,
        )
        sums_out[pl.ds(n * deep, deep), :] = jnp.dot(
            hot, shifted_rows[...], preferred_element_type=jnp.float32
        ).astype(jnp.bfloat16)
        sum_copy(n).start()
        return carry

    def send(g, carry):
        matched_group(g * mgroup)

        @pl.when(g == 0)
        def _():
            pl.semaphore_wait(barrier, owners - 1)
            lax.fori_loop(1, owners, tell, 0)
            heard[me] = info[me]

        def start(i, carry):
            patch, dest, passed = turn(i)

            @pl.when((dest != me) & passed)
            def _():
                pass_copy(patch, dest, local).start()

            @pl.when((dest != me) & jnp.logical_not(passed))
            def _():
                data_copy(patch, dest, me).start()

            @pl.when((dest == me) & passed)
            def _():
                passing[local] = outgoing[patch]

            return carry

        last_held = 2 * each // mgroup - 1
        held = (inner == 0) & (g >= each // mgroup) & (g <= last_held)

        @pl.when(jnp.logical_not(held))
        def _():
            lax.fori_loop(g * mgroup, (g + 1) * mgroup, start, 0)

        @pl.when(held & (g == last_held))
        def _():
            def gone(i, carry):
                patch, dest, _ = turn(i)
                pass_copy(patch, dest, local).wait_send()
                return carry

            lax.fori_loop(0, each, gone, 0)
            lax.fori_loop(each, 2 * each, start, 0)

        return carry

    lax.fori_loop(0, owners // mgroup, send, 0)
    arrived[me] = outgoing[me]
    pltpu.make_async_copy(heard.at[others], heard.at[others], sems.at[1]).wait()

    @pl.when(inner == 1)
    def _():
        lax.fori_loop(0, span * ncol // group, pass_shift, 0)
        lax.fori_loop(0, pieces, send_sum, 0)


    wide = lax.broadcasted_iota(jnp.int32, (owners, PATCH), 1)
    entries = weights.shape[1]
    letters = jnp.concatenate([heard[o, 0:1, :] for o in range(owners)], axis=0)
    depth = jnp.zeros((PATCH, PATCH), jnp.float32)
    for j in range(CAP):
        live, entry, top, left = (letters[:, 4 * j + n : 4 * j + n + 1] for n in range(4))
        hits = lax.broadcasted_iota(jnp.int32, (owners, entries), 1) == entry
        weight = jnp.sum(jnp.where(hits, weights[...], 0.0), axis=1, keepdims=True)
        weight = jnp.where(live > 0, weight, 0.0)
        row_weight = jnp.where((wide >= top) & (wide < top + rows), weight, 0.0)
        col_cover = jnp.where((wide >= left) & (wide < left + cols), 1.0, 0.0)
        depth = depth + lax.dot_general(
            row_weight.astype(jnp.bfloat16),
            col_cover.astype(jnp.bfloat16),
            (((0,), (0,)), ((), ())),
            preferred_element_type=jnp.float32,
        )
    coadd[...] = jnp.maximum(depth, 1.0)

    down = lax.broadcasted_iota(jnp.int32, (PATCH, many * rows), 0)

    def gather(source, limit):
        def step(g, carry):
            origins = [source(g * group + n) for n in range(group)]
            for n, origin in enumerate(origins):

                @pl.when(g * group + n < limit)
                def _():
                    data_copy(origin, origin, origin).wait_recv()

            shifted, target = shift_group(origins, 0, arrived, origins)
            hot = jnp.where(down == target, 1.0, 0.0).astype(jnp.bfloat16)
            total[...] += jnp.dot(hot, shifted, preferred_element_type=jnp.float32)
            return carry

        lax.fori_loop(0, span * ncol // group, step, 0)

    @pl.when(inner == 1)
    def _():
        gather(far_source, span * ncol)

    gather(near_source, span * ncol - 1)

    @pl.when(inner == 0)
    def _():
        for n in range(pieces):
            sum_copy(n).wait_recv()
        total[...] += sums_in[...].astype(jnp.float32)

    coadd[...] = total[...] / coadd[...]

    first_rows, last_rows = pl.ds(0, HALO), pl.ds(PATCH - HALO, HALO)
    first, last, whole = pl.ds(0, LANES), pl.ds(PATCH - LANES, LANES), pl.ds(0, PATCH)
    left_tile, right_tile = pl.ds(PATCH, LANES), pl.ds(PATCH + LANES, LANES)
    below = pl.ds(HALO, HALO)
    moves = (
        (1, 0, coadd.at[last_rows, whole], halo.at[first_rows, whole]),
        (-1, 0, coadd.at[first_rows, whole], halo.at[below, whole]),
        (1, 1, coadd.at[last_rows, last], halo.at[first_rows, left_tile]),
        (1, -1, coadd.at[last_rows, first], halo.at[first_rows, right_tile]),
        (-1, 1, coadd.at[first_rows, last], halo.at[below, left_tile]),
        (-1, -1, coadd.at[first_rows, first], halo.at[below, right_tile]),
        (0, -1, image.at[below, whole], image.at[pl.ds(PATCH + HALO, HALO), whole]),
        (0, 1, image.at[pl.ds(PATCH, HALO), whole], image.at[first_rows, whole]),
    )

    def inside(dp, dc):
        row, col = prow + dp, pcol + dc
        return (row >= 0) & (row < nrow) & (col >= 0) & (col < ncol)

    def halo_copy(n):
        dp, dc, origin, target = moves[n]
        return pltpu.make_async_remote_copy(
            src_ref=origin,
            dst_ref=target,
            send_sem=halo_sems.at[0, n],
            recv_sem=halo_sems.at[1, n],
            device_id=(prow + dp, pcol + dc),
            device_id_type=MESH,
        )

    for n, (dp, dc, _, _) in enumerate(moves):
        if dp == 0 and dc < 0:
            image[HALO : HALO + PATCH, 0:PATCH] = coadd[...].T

        @pl.when(inside(dp, dc))
        def _():
            halo_copy(n).start()

    def sent(i, carry):
        patch, dest, passed = turn(i)
        gone = passed & (inner == 0)

        @pl.when((dest != me) & jnp.logical_not(gone))
        def _():
            data_copy(patch, dest, me).wait_send()

        return carry

    lax.fori_loop(0, owners, sent, 0)

    @pl.when(inner == 1)
    def _():
        for n in range(pieces):
            sum_copy(n).wait_send()

    pltpu.make_async_copy(info.at[others], info.at[others], sems.at[0]).wait()

    reach = taps.shape[1]
    at_sub = lax.broadcasted_iota(jnp.int32, (reach, reach), 0)
    at_lane = lax.broadcasted_iota(jnp.int32, (reach, reach), 1)
    tap_column = jnp.sum(jnp.where(at_sub == at_lane, taps[...], 0.0), axis=1, keepdims=True)

    def band(shift):
        at_sub = lax.broadcasted_iota(jnp.int32, (reach, WIDE), 0)
        at_lane = lax.broadcasted_iota(jnp.int32, (reach, WIDE), 1)
        origin = jnp.sum(
            jnp.where(at_lane == (at_sub + 1 - shift + WIDE) % WIDE, tap_column, 0.0),
            axis=0,
            keepdims=True,
        )
        origin = jnp.broadcast_to(origin, (PATCH, WIDE))
        return pltpu.roll(origin, 0, 1, stride=1, stride_axis=0)

    across = band(0)
    lane = lax.broadcasted_iota(jnp.int32, (PATCH, LANES), 1)
    edges = jnp.where(
        lane < HALO,
        across[:, 0:LANES],
        jnp.where(lane < 2 * HALO, across[:, PATCH:], 0.0),
    )
    along = jnp.concatenate([band(HALO)[:, 0:PATCH], edges], axis=1)

    for n, (dp, dc, _, _) in enumerate(moves):

        @pl.when(inside(dp, dc))
        def _():
            halo_copy(n).wait_send()

        @pl.when(inside(-dp, -dc))
        def _():
            halo_copy(n).wait_recv()

    turned = halo[...].T
    image[HALO : HALO + PATCH, PATCH:] = turned[0:PATCH, :]
    image[0:HALO, PATCH:] = turned[PATCH + LANES - HALO : PATCH + LANES, :]
    image[PATCH + HALO : PATCH + 2 * HALO, PATCH:] = turned[PATCH + LANES : PATCH + LANES + HALO, :]
    partial = half_dot(across, image[...], ((1,), (0,)))
    detection[...] = half_dot(along, partial, ((1,), (1,)))


def finish(coadd, detection, coadd_out, detection_out, sems):
    first = pltpu.make_async_copy(coadd, coadd_out, sems.at[0])
    second = pltpu.make_async_copy(detection, detection_out, sems.at[1])
    first.start()
    second.start()
    first.wait()
    second.wait()


def shards(
    blocks,
    owner,
    row_offset,
    col_offset,
    exposure,
    basis_rows,
    basis_cols,
    coef_table,
    weight_table,
    det_taps,
):
    nrow = lax.axis_size("prow")
    ncol = lax.axis_size("pcol")
    owners = nrow * ncol
    count, rows, cols = blocks.shape
    kinds, taps = basis_rows.shape
    slots = owners * CAP
    span = nrow // 2
    vmem = pl.BlockSpec(memory_space=pltpu.VMEM)
    anywhere = pl.BlockSpec(memory_space=pl.ANY)
    small = (
        owner.reshape(1, count),
        exposure[None],
        row_offset[None],
        col_offset[None],
        weight_table[None],
        coef_table.T,
        basis_rows,
        basis_cols,
        det_taps[None],
    )

    tract = jax.ShapeDtypeStruct((PATCH, PATCH), jnp.float32)
    even = kinds + kinds % 2
    coadd, detection = pl.pallas_call(
        functools.partial(whole_kernel, nrow, ncol),
        out_shape=(pltpu.VMEM((PATCH, PATCH), jnp.float32),) * 2,
        in_specs=[tuple(anywhere for _ in small), anywhere],
        out_specs=(vmem, vmem),
        scratch_shapes=[
            tuple(pltpu.VMEM(x.shape, x.dtype) for x in small),
            pltpu.VMEM((count, rows, cols), jnp.bfloat16),
            pltpu.VMEM((1, slots), jnp.int32),
            pltpu.SMEM((1, slots), jnp.int32),
            pltpu.VMEM((owners, 2, LANES), jnp.int32),
            pltpu.VMEM((slots, kinds * cols), jnp.float32),
            pltpu.VMEM((cols, kinds * cols), jnp.bfloat16),
            pltpu.VMEM((rows, even * rows), jnp.bfloat16),
            pltpu.VMEM((kinds * rows, MGROUP * CAP * cols), jnp.bfloat16),
            pltpu.VMEM((owners, CAP * rows, cols), jnp.bfloat16),
            pltpu.VMEM((owners, CAP * rows, cols), jnp.bfloat16),
            pltpu.VMEM((span * ncol, CAP * rows, cols), jnp.bfloat16),
            pltpu.VMEM((span * ncol * CAP * rows, PATCH), jnp.bfloat16),
            pltpu.VMEM((span * ncol // GROUP, 1, GROUP * CAP * rows), jnp.int32),
            pltpu.VMEM((PATCH, PATCH), jnp.bfloat16),
            pltpu.VMEM((PATCH, PATCH), jnp.bfloat16),
            pltpu.VMEM((owners, 2, LANES), jnp.int32),
            pltpu.VMEM((PATCH, PATCH), jnp.float32),
            pltpu.VMEM((WIDE, WIDE), jnp.float32),
            pltpu.VMEM((LANES, PATCH + 2 * LANES), jnp.float32),
            pltpu.SemaphoreType.DMA((4,)),
            pltpu.SemaphoreType.DMA((2, owners)),
            pltpu.SemaphoreType.DMA((2, 8)),
            pltpu.SemaphoreType.DMA((span * ncol,)),
            pltpu.SemaphoreType.DMA((2, PIECES)),
            pltpu.SemaphoreType.DMA((len(small),)),
        ],
        compiler_params=pltpu.CompilerParams(
            collective_id=0, has_side_effects=True, vmem_limit_bytes=56 * 1024 * 1024
        ),
        name="whole",
    )(small, blocks)
    return pl.pallas_call(
        finish,
        out_shape=(tract, tract),
        in_specs=[vmem] * 2,
        out_specs=(pl.BlockSpec(memory_space=pl.ANY),) * 2,
        scratch_shapes=[pltpu.SemaphoreType.DMA((2,))],
        compiler_params=pltpu.CompilerParams(vmem_limit_bytes=2 * 1024 * 1024),
        name="finish",
    )(coadd, detection)


def solution(mesh):
    in_specs = (
        P(("prow", "pcol"), None, None),
        P(("prow", "pcol"), None),
        P(("prow", "pcol")),
        P(("prow", "pcol")),
        P(("prow", "pcol")),
        P(),
        P(),
        P(),
        P(),
        P(),
    )
    out_specs = (P("prow", "pcol"), P("prow", "pcol"))
    return jax.shard_map(shards, mesh=mesh, in_specs=in_specs, out_specs=out_specs, check_vma=False)
```

```python
import functools

import jax
import jax.numpy as jnp
from jax import lax
from jax.experimental import pallas as pl
from jax.experimental.pallas import tpu as pltpu
from jax.sharding import PartitionSpec as P

DET_R = 15
PATCH = 384
CAP = 2
LANES = 128
MESH = pl.DeviceIdType.MESH
EXACT = lax.Precision.HIGHEST


HALO = 16
MGROUP = 2
GROUP = 8
PIECES = 3
WIDE = 512


def half_dot(left, right, dims):
    return lax.dot_general(
        left.astype(jnp.bfloat16),
        right.astype(jnp.bfloat16),
        (dims, ((), ())),
        preferred_element_type=jnp.float32,
    )


def prepare(kinds, owner, exposure, row_offset, col_offset, weights, coef_table, picks_out, told_out, coef_out):
    count = owner.shape[1]
    entries = weights.shape[1]
    slots = coef_out.shape[0]
    owners = slots // CAP
    at_sub = lax.broadcasted_iota(jnp.int32, (count, count), 0)
    at_lane = lax.broadcasted_iota(jnp.int32, (count, count), 1)

    def column(row):
        spread = jnp.broadcast_to(row, (count, count))
        return jnp.sum(jnp.where(at_sub == at_lane, spread, 0), axis=1, keepdims=True)

    same = jnp.where((column(owner[...]) == owner[...]) & (at_sub < at_lane), 1, 0)
    slot = owner[...] * CAP + jnp.sum(same, axis=0, keepdims=True)
    at_slot = lax.broadcasted_iota(jnp.int32, (count, slots), 1) == column(slot)
    numbers = lax.broadcasted_iota(jnp.int32, (count, slots), 0)
    picks_out[...] = jnp.sum(jnp.where(at_slot, numbers, 0), axis=0, keepdims=True)
    lane = lax.broadcasted_iota(jnp.int32, (owners, LANES), 1)
    told = jnp.zeros((owners, LANES), jnp.int32)
    for j in range(CAP):
        own = lax.broadcasted_iota(jnp.int32, (owners, count), 0) * CAP + j == slot
        values = (jnp.ones_like(slot), exposure[...], row_offset[...], col_offset[...])
        for n, value in enumerate(values):
            found = jnp.sum(jnp.where(own, value, 0), axis=1, keepdims=True)
            told = jnp.where(lane == 4 * j + n, found, told)
    for o in range(owners):
        mate = (o + owners // 2) % owners
        told_out[o, 0:1, :] = told[o : o + 1, :]
        told_out[o, 1:2, :] = told[mate : mate + 1, :]
    own = lax.broadcasted_iota(jnp.int32, (slots, count), 0) == slot
    index = jnp.sum(jnp.where(own, exposure[...], 0), axis=1, keepdims=True)
    hits = lax.broadcasted_iota(jnp.int32, (slots, entries), 1) == index
    weight = jnp.sum(jnp.where(hits, weights[...], 0.0), axis=1, keepdims=True)
    weight = weight.astype(jnp.bfloat16).astype(jnp.float32)
    cols = coef_out.shape[1] // kinds
    coefs = lax.dot_general(
        hits.astype(jnp.float32),
        coef_table[...],
        (((1,), (1,)), ((), ())),
        precision=EXACT,
        preferred_element_type=jnp.float32,
    )
    coefs = coefs * weight
    for k in range(kinds):
        coef_out[:, k * cols : (k + 1) * cols] = jnp.broadcast_to(
            coefs[:, k : k + 1], (slots, cols)
        )


def build_tables(basis_rows, basis_cols, col_out, row_out):
    kinds, taps = basis_rows.shape
    half = taps // 2
    rows, cols = row_out.shape[0], col_out.shape[0]
    tap = lax.broadcasted_iota(jnp.int32, (taps, LANES), 0)
    lane = lax.broadcasted_iota(jnp.int32, (taps, LANES), 1)

    def spread(value, target):
        hot = jnp.where(lane == (target + LANES) % LANES, 1.0, 0.0).astype(jnp.bfloat16)
        return jnp.dot(value[...], hot, preferred_element_type=jnp.float32)

    col_src = spread(basis_cols, half - tap)
    even = spread(basis_rows, tap - half)
    odd = spread(basis_rows, tap - half + rows)
    near = jnp.abs(
        lax.broadcasted_iota(jnp.int32, (cols, LANES), 1)
        - lax.broadcasted_iota(jnp.int32, (cols, LANES), 0)
    )
    for k in range(kinds):
        source = jnp.broadcast_to(col_src[k : k + 1, :], (cols, LANES))
        rolled = pltpu.roll(source, 0, 1, stride=1, stride_axis=0)
        col_out[:, k * LANES : (k + 1) * LANES] = jnp.where(near <= half, rolled, 0.0).astype(
            jnp.bfloat16
        )
    near = jnp.abs(
        lax.broadcasted_iota(jnp.int32, (rows, LANES), 1) % rows
        - lax.broadcasted_iota(jnp.int32, (rows, LANES), 0)
    )
    for k in range(0, kinds, 2):
        source = even[k : k + 1, :]
        if k + 1 < kinds:
            source = source + odd[k + 1 : k + 2, :]
        rolled = pltpu.roll(
            jnp.broadcast_to(source, (rows, LANES)), 0, 1, stride=1, stride_axis=0
        )
        row_out[:, k * rows : k * rows + LANES] = jnp.where(near <= half, rolled, 0.0).astype(
            jnp.bfloat16
        )


def whole_kernel(
    nrow,
    ncol,
    small_sources,
    source_blocks,
    coadd,
    partial,
    along,
    small,
    blocks,
    pick_row,
    picks,
    info,
    coefs,
    col_table,
    row_table,
    sections,
    outgoing,
    arrived,
    passing,
    shifted_rows,
    shifted_to,
    sums_out,
    sums_in,
    heard,
    total,
    image,
    halo,
    sems,
    data_sems,
    halo_sems,
    pass_sems,
    sum_sems,
    load_sems,
):
    owner, exposure, row_offset, col_offset, weights, coef_table, basis_rows, basis_cols, taps = small
    owners = nrow * ncol
    prow, pcol = lax.axis_index("prow"), lax.axis_index("pcol")
    me = prow * ncol + pcol
    rows, cols = blocks.shape[1:]
    kinds = basis_rows.shape[0]
    span = nrow // 2
    half = span // 2
    each = half * ncol
    side, level = prow // span, prow % span
    inner = (level // half + side) % 2
    mate = (prow + span) % nrow
    local = level * ncol + pcol

    def turn(i):
        phase, j = i // each, i % each
        col = (pcol + 1 + i) % ncol
        across = (level + 1 + j // ncol) % half
        passed = phase == inner
        direct = phase == 1 - inner
        at = jnp.where(passed, (1 - side) * half + across, side * half + across)
        at = jnp.where(phase < 2, at, (level + 1 + (i - 2 * each) // ncol) % span)
        patch = (jnp.where(phase < 2, 1 - side, side) * span + at) * ncol + col
        dest = (jnp.where(direct, 1 - side, side) * span + at) * ncol + col
        return patch, dest, passed

    def far_source(i):
        at = (side * half + i // ncol) % span
        return ((1 - side) * span + at) * ncol + (pcol + 2 * ncol - 1 - i % ncol) % ncol

    def near_source(i):
        at = (level + 2 * span - 1 - i // ncol) % span
        return (side * span + at) * ncol + (pcol + 2 * ncol - 1 - i % ncol) % ncol

    def place(device):
        return (device // ncol, device % ncol)

    barrier = pltpu.get_barrier_semaphore()
    loads = [
        pltpu.make_async_copy(source, target, load_sems.at[n])
        for n, (source, target) in enumerate(zip(small_sources, small))
    ]
    for load in loads:
        load.start()
    load_blocks = pltpu.make_async_copy(source_blocks, blocks, sems.at[3])
    load_blocks.start()

    def greet(i, carry):
        other = lax.rem(me + i, owners)
        pl.semaphore_signal(barrier, inc=1, device_id=place(other), device_id_type=MESH)
        return carry

    lax.fori_loop(1, owners, greet, 0)
    halo[...] = jnp.zeros_like(halo)
    image[0:HALO, :] = jnp.zeros((HALO, WIDE), jnp.float32)
    image[PATCH + HALO :, :] = jnp.zeros((WIDE - PATCH - HALO, WIDE), jnp.float32)
    total[...] = jnp.zeros_like(total)
    for load in loads:
        load.wait()
    prepare(
        kinds, owner, exposure, row_offset, col_offset, weights, coef_table, pick_row, info, coefs
    )
    lift = pltpu.make_async_copy(pick_row, picks, sems.at[2])
    lift.start()
    build_tables(basis_rows, basis_cols, col_table, row_table)
    lift.wait()
    load_blocks.wait()

    def tell(i, carry):
        other = lax.rem(me + i, owners)
        pltpu.make_async_remote_copy(
            src_ref=info.at[other],
            dst_ref=heard.at[me],
            send_sem=sems.at[0],
            recv_sem=sems.at[1],
            device_id=place(other),
            device_id_type=MESH,
        ).start()
        return carry

    others = pl.ds(0, owners - 1)

    mgroup = MGROUP

    def matched_group(first):
        slots_of = [
            turn(first + n)[0] * CAP + j for n in range(mgroup) for j in range(CAP)
        ]
        pixels = jnp.concatenate([blocks[picks[0, s]] for s in slots_of], axis=0)
        coefs_of = [coefs[pl.ds(s, 1), :] for s in slots_of]
        section = jnp.dot(pixels, col_table[...], preferred_element_type=jnp.float32)
        for k in range(kinds):
            for n, coef in enumerate(coefs_of):
                part = section[n * rows : (n + 1) * rows, k * cols : (k + 1) * cols]
                sections[k * rows : (k + 1) * rows, n * cols : (n + 1) * cols] = (
                    coef[:, k * cols : (k + 1) * cols] * part
                ).astype(jnp.bfloat16)
        matched = jnp.dot(
            row_table[:, 0 : kinds * rows], sections[...], preferred_element_type=jnp.float32
        ).astype(jnp.bfloat16)
        for n in range(mgroup):
            for j in range(CAP):
                m = n * CAP + j
                outgoing[turn(first + n)[0], j * rows : (j + 1) * rows, :] = matched[
                    :, m * cols : (m + 1) * cols
                ]

    def data_copy(patch, dest, origin):
        return pltpu.make_async_remote_copy(
            src_ref=outgoing.at[patch],
            dst_ref=arrived.at[origin],
            send_sem=data_sems.at[0, patch],
            recv_sem=data_sems.at[1, origin],
            device_id=place(dest),
            device_id_type=MESH,
        )

    def pass_copy(patch, dest, origin):
        return pltpu.make_async_remote_copy(
            src_ref=outgoing.at[patch],
            dst_ref=passing.at[origin],
            send_sem=data_sems.at[0, patch],
            recv_sem=pass_sems.at[origin],
            device_id=place(dest),
            device_id_type=MESH,
        )

    pieces = sum_sems.shape[1]
    deep = PATCH // pieces

    def sum_copy(n):
        piece = pl.ds(n * deep, deep)
        return pltpu.make_async_remote_copy(
            src_ref=sums_out.at[piece],
            dst_ref=sums_in.at[piece],
            send_sem=sum_sems.at[0, n],
            recv_sem=sum_sems.at[1, n],
            device_id=(mate, pcol),
            device_id_type=MESH,
        )

    offset = lax.broadcasted_iota(jnp.int32, (cols, PATCH), 1) - lax.broadcasted_iota(
        jnp.int32, (cols, PATCH), 0
    )
    group = GROUP
    many = group * CAP

    def shift_group(origins, which, buffer, slots_at):
        lane = lax.broadcasted_iota(jnp.int32, (1, many * rows), 1)
        target = lane % rows
        shifted = []
        for n, origin in enumerate(origins):
            letter = heard[origin, which : which + 1, :]
            for j in range(CAP):
                live, _, top, left = (letter[:, 4 * j + m : 4 * j + m + 1] for m in range(4))
                left = jnp.where(live > 0, left, -PATCH)
                hot = jnp.where(offset == left, 1.0, 0.0).astype(jnp.bfloat16)
                block = buffer[slots_at[n], j * rows : (j + 1) * rows, :]
                shifted.append(
                    jnp.dot(block, hot, preferred_element_type=jnp.float32).astype(jnp.bfloat16)
                )
                target = target + jnp.where(lane // rows == n * CAP + j, top, 0)
        return jnp.concatenate(shifted, axis=0), target

    def pass_shift(g, carry):
        slots_at, origins = [], []
        for n in range(group):
            i = g * group + n
            origin = near_source(i)
            slot = origin % (span * ncol)

            @pl.when(i < span * ncol - 1)
            def _():
                pass_copy(origin, origin, slot).wait_recv()

            slots_at.append(slot)
            origins.append(origin)
        shifted, target = shift_group(origins, 1, passing, slots_at)
        shifted_rows[pl.ds(g * many * rows, many * rows), :] = shifted
        shifted_to[g] = target
        return carry

    def send_sum(n, carry):
        down = lax.broadcasted_iota(jnp.int32, (deep, many * rows), 0) + n * deep
        hot = jnp.concatenate(
            [
                jnp.where(down == shifted_to[g], 1.0, 0.0).astype(jnp.bfloat16)
                for g in range(span * ncol // group)
            ],
            axis=1,
        )
        sums_out[pl.ds(n * deep, deep), :] = jnp.dot(
            hot, shifted_rows[...], preferred_element_type=jnp.float32
        ).astype(jnp.bfloat16)
        sum_copy(n).start()
        return carry

    def send(g, carry):
        matched_group(g * mgroup)

        @pl.when(g == 0)
        def _():
            pl.semaphore_wait(barrier, owners - 1)
            lax.fori_loop(1, owners, tell, 0)
            heard[me] = info[me]

        def start(i, carry):
            patch, dest, passed = turn(i)

            @pl.when((dest != me) & passed)
            def _():
                pass_copy(patch, dest, local).start()

            @pl.when((dest != me) & jnp.logical_not(passed))
            def _():
                data_copy(patch, dest, me).start()

            @pl.when((dest == me) & passed)
            def _():
                passing[local] = outgoing[patch]

            return carry

        last_held = 2 * each // mgroup - 1
        held = (inner == 0) & (g >= each // mgroup) & (g <= last_held)

        @pl.when(jnp.logical_not(held))
        def _():
            lax.fori_loop(g * mgroup, (g + 1) * mgroup, start, 0)

        @pl.when(held & (g == last_held))
        def _():
            def gone(i, carry):
                patch, dest, _ = turn(i)
                pass_copy(patch, dest, local).wait_send()
                return carry

            lax.fori_loop(0, each, gone, 0)
            lax.fori_loop(each, 2 * each, start, 0)

        return carry

    lax.fori_loop(0, owners // mgroup, send, 0)
    arrived[me] = outgoing[me]
    pltpu.make_async_copy(heard.at[others], heard.at[others], sems.at[1]).wait()

    @pl.when(inner == 1)
    def _():
        lax.fori_loop(0, span * ncol // group, pass_shift, 0)
        lax.fori_loop(0, pieces, send_sum, 0)


    wide = lax.broadcasted_iota(jnp.int32, (owners, PATCH), 1)
    entries = weights.shape[1]
    letters = jnp.concatenate([heard[o, 0:1, :] for o in range(owners)], axis=0)
    depth = jnp.zeros((PATCH, PATCH), jnp.float32)
    for j in range(CAP):
        live, entry, top, left = (letters[:, 4 * j + n : 4 * j + n + 1] for n in range(4))
        hits = lax.broadcasted_iota(jnp.int32, (owners, entries), 1) == entry
        weight = jnp.sum(jnp.where(hits, weights[...], 0.0), axis=1, keepdims=True)
        weight = jnp.where(live > 0, weight, 0.0)
        row_weight = jnp.where((wide >= top) & (wide < top + rows), weight, 0.0)
        col_cover = jnp.where((wide >= left) & (wide < left + cols), 1.0, 0.0)
        depth = depth + lax.dot_general(
            row_weight.astype(jnp.bfloat16),
            col_cover.astype(jnp.bfloat16),
            (((0,), (0,)), ((), ())),
            preferred_element_type=jnp.float32,
        )
    coadd[...] = jnp.maximum(depth, 1.0)

    down = lax.broadcasted_iota(jnp.int32, (PATCH, many * rows), 0)

    def gather(source, limit):
        def step(g, carry):
            origins = [source(g * group + n) for n in range(group)]
            for n, origin in enumerate(origins):

                @pl.when(g * group + n < limit)
                def _():
                    data_copy(origin, origin, origin).wait_recv()

            shifted, target = shift_group(origins, 0, arrived, origins)
            hot = jnp.where(down == target, 1.0, 0.0).astype(jnp.bfloat16)
            total[...] += jnp.dot(hot, shifted, preferred_element_type=jnp.float32)
            return carry

        lax.fori_loop(0, span * ncol // group, step, 0)

    @pl.when(inner == 1)
    def _():
        gather(far_source, span * ncol)

    gather(near_source, span * ncol - 1)

    @pl.when(inner == 0)
    def _():
        for n in range(pieces):
            sum_copy(n).wait_recv()
            piece = pl.ds(n * deep, deep)
            total[piece, :] += sums_in[piece, :].astype(jnp.float32)

    coadd[...] = total[...] / coadd[...]

    first_rows, last_rows = pl.ds(0, HALO), pl.ds(PATCH - HALO, HALO)
    first, last, whole = pl.ds(0, LANES), pl.ds(PATCH - LANES, LANES), pl.ds(0, PATCH)
    left_tile, right_tile = pl.ds(PATCH, LANES), pl.ds(PATCH + LANES, LANES)
    below = pl.ds(HALO, HALO)
    moves = (
        (1, 0, coadd.at[last_rows, whole], halo.at[first_rows, whole]),
        (-1, 0, coadd.at[first_rows, whole], halo.at[below, whole]),
        (1, 1, coadd.at[last_rows, last], halo.at[first_rows, left_tile]),
        (1, -1, coadd.at[last_rows, first], halo.at[first_rows, right_tile]),
        (-1, 1, coadd.at[first_rows, last], halo.at[below, left_tile]),
        (-1, -1, coadd.at[first_rows, first], halo.at[below, right_tile]),
        (0, -1, image.at[below, whole], image.at[pl.ds(PATCH + HALO, HALO), whole]),
        (0, 1, image.at[pl.ds(PATCH, HALO), whole], image.at[first_rows, whole]),
    )

    def inside(dp, dc):
        row, col = prow + dp, pcol + dc
        return (row >= 0) & (row < nrow) & (col >= 0) & (col < ncol)

    def halo_copy(n):
        dp, dc, origin, target = moves[n]
        return pltpu.make_async_remote_copy(
            src_ref=origin,
            dst_ref=target,
            send_sem=halo_sems.at[0, n],
            recv_sem=halo_sems.at[1, n],
            device_id=(prow + dp, pcol + dc),
            device_id_type=MESH,
        )

    for n, (dp, dc, _, _) in enumerate(moves):
        if dp == 0 and dc < 0:
            image[HALO : HALO + PATCH, 0:PATCH] = coadd[...].T

        @pl.when(inside(dp, dc))
        def _():
            halo_copy(n).start()

    def sent(i, carry):
        patch, dest, passed = turn(i)
        gone = passed & (inner == 0)

        @pl.when((dest != me) & jnp.logical_not(gone))
        def _():
            data_copy(patch, dest, me).wait_send()

        return carry

    lax.fori_loop(0, owners, sent, 0)

    @pl.when(inner == 1)
    def _():
        for n in range(pieces):
            sum_copy(n).wait_send()

    pltpu.make_async_copy(info.at[others], info.at[others], sems.at[0]).wait()

    reach = taps.shape[1]
    at_sub = lax.broadcasted_iota(jnp.int32, (reach, reach), 0)
    at_lane = lax.broadcasted_iota(jnp.int32, (reach, reach), 1)
    tap_column = jnp.sum(jnp.where(at_sub == at_lane, taps[...], 0.0), axis=1, keepdims=True)

    def band(shift):
        at_sub = lax.broadcasted_iota(jnp.int32, (reach, WIDE), 0)
        at_lane = lax.broadcasted_iota(jnp.int32, (reach, WIDE), 1)
        origin = jnp.sum(
            jnp.where(at_lane == (at_sub + 1 - shift + WIDE) % WIDE, tap_column, 0.0),
            axis=0,
            keepdims=True,
        )
        origin = jnp.broadcast_to(origin, (PATCH, WIDE))
        return pltpu.roll(origin, 0, 1, stride=1, stride_axis=0)

    across = band(0)
    lane = lax.broadcasted_iota(jnp.int32, (PATCH, LANES), 1)
    edges = jnp.where(
        lane < HALO,
        across[:, 0:LANES],
        jnp.where(lane < 2 * HALO, across[:, PATCH:], 0.0),
    )
    along[...] = jnp.concatenate([band(HALO)[:, 0:PATCH], edges], axis=1).astype(jnp.bfloat16)

    for n, (dp, dc, _, _) in enumerate(moves):

        @pl.when(inside(dp, dc))
        def _():
            halo_copy(n).wait_send()

        @pl.when(inside(-dp, -dc))
        def _():
            halo_copy(n).wait_recv()

    turned = halo[...].T
    image[HALO : HALO + PATCH, PATCH:] = turned[0:PATCH, :]
    image[0:HALO, PATCH:] = turned[PATCH + LANES - HALO : PATCH + LANES, :]
    image[PATCH + HALO : PATCH + 2 * HALO, PATCH:] = turned[PATCH + LANES : PATCH + LANES + HALO, :]
    partial[...] = half_dot(across, image[...], ((1,), (0,))).astype(jnp.bfloat16)


def finish(coadd, partial, along, coadd_out, detection_out, detection, sems):
    first = pltpu.make_async_copy(coadd, coadd_out, sems.at[0])
    first.start()
    steps = sems.shape[0] - 1
    moves = []
    for n in range(steps):
        piece = pl.ds(n * (PATCH // steps), PATCH // steps)
        detection[piece, :] = half_dot(along[piece, :], partial[...], ((1,), (1,)))
        moves.append(
            pltpu.make_async_copy(detection.at[piece], detection_out.at[piece], sems.at[n + 1])
        )
        moves[-1].start()
    first.wait()
    for move in moves:
        move.wait()


def shards(
    blocks,
    owner,
    row_offset,
    col_offset,
    exposure,
    basis_rows,
    basis_cols,
    coef_table,
    weight_table,
    det_taps,
):
    nrow = lax.axis_size("prow")
    ncol = lax.axis_size("pcol")
    owners = nrow * ncol
    count, rows, cols = blocks.shape
    kinds, taps = basis_rows.shape
    slots = owners * CAP
    span = nrow // 2
    vmem = pl.BlockSpec(memory_space=pltpu.VMEM)
    anywhere = pl.BlockSpec(memory_space=pl.ANY)
    small = (
        owner.reshape(1, count),
        exposure[None],
        row_offset[None],
        col_offset[None],
        weight_table[None],
        coef_table.T,
        basis_rows,
        basis_cols,
        det_taps[None],
    )

    tract = jax.ShapeDtypeStruct((PATCH, PATCH), jnp.float32)
    even = kinds + kinds % 2
    coadd, partial, along = pl.pallas_call(
        functools.partial(whole_kernel, nrow, ncol),
        out_shape=(
            pltpu.VMEM((PATCH, PATCH), jnp.float32),
            pltpu.VMEM((PATCH, WIDE), jnp.bfloat16),
            pltpu.VMEM((PATCH, WIDE), jnp.bfloat16),
        ),
        in_specs=[tuple(anywhere for _ in small), anywhere],
        out_specs=(vmem, vmem, vmem),
        scratch_shapes=[
            tuple(pltpu.VMEM(x.shape, x.dtype) for x in small),
            pltpu.VMEM((count, rows, cols), jnp.bfloat16),
            pltpu.VMEM((1, slots), jnp.int32),
            pltpu.SMEM((1, slots), jnp.int32),
            pltpu.VMEM((owners, 2, LANES), jnp.int32),
            pltpu.VMEM((slots, kinds * cols), jnp.float32),
            pltpu.VMEM((cols, kinds * cols), jnp.bfloat16),
            pltpu.VMEM((rows, even * rows), jnp.bfloat16),
            pltpu.VMEM((kinds * rows, MGROUP * CAP * cols), jnp.bfloat16),
            pltpu.VMEM((owners, CAP * rows, cols), jnp.bfloat16),
            pltpu.VMEM((owners, CAP * rows, cols), jnp.bfloat16),
            pltpu.VMEM((span * ncol, CAP * rows, cols), jnp.bfloat16),
            pltpu.VMEM((span * ncol * CAP * rows, PATCH), jnp.bfloat16),
            pltpu.VMEM((span * ncol // GROUP, 1, GROUP * CAP * rows), jnp.int32),
            pltpu.VMEM((PATCH, PATCH), jnp.bfloat16),
            pltpu.VMEM((PATCH, PATCH), jnp.bfloat16),
            pltpu.VMEM((owners, 2, LANES), jnp.int32),
            pltpu.VMEM((PATCH, PATCH), jnp.float32),
            pltpu.VMEM((WIDE, WIDE), jnp.float32),
            pltpu.VMEM((LANES, PATCH + 2 * LANES), jnp.float32),
            pltpu.SemaphoreType.DMA((4,)),
            pltpu.SemaphoreType.DMA((2, owners)),
            pltpu.SemaphoreType.DMA((2, 8)),
            pltpu.SemaphoreType.DMA((span * ncol,)),
            pltpu.SemaphoreType.DMA((2, PIECES)),
            pltpu.SemaphoreType.DMA((len(small),)),
        ],
        compiler_params=pltpu.CompilerParams(
            collective_id=0, has_side_effects=True, vmem_limit_bytes=56 * 1024 * 1024
        ),
        name="whole",
    )(small, blocks)
    return pl.pallas_call(
        finish,
        out_shape=(tract, tract),
        in_specs=[vmem] * 3,
        out_specs=(pl.BlockSpec(memory_space=pl.ANY),) * 2,
        scratch_shapes=[
            pltpu.VMEM((PATCH, PATCH), jnp.float32),
            pltpu.SemaphoreType.DMA((4,)),
        ],
        compiler_params=pltpu.CompilerParams(vmem_limit_bytes=8 * 1024 * 1024),
        name="finish",
    )(coadd, partial, along)


def solution(mesh):
    in_specs = (
        P(("prow", "pcol"), None, None),
        P(("prow", "pcol"), None),
        P(("prow", "pcol")),
        P(("prow", "pcol")),
        P(("prow", "pcol")),
        P(),
        P(),
        P(),
        P(),
        P(),
    )
    out_specs = (P("prow", "pcol"), P("prow", "pcol"))
    return jax.shard_map(shards, mesh=mesh, in_specs=in_specs, out_specs=out_specs, check_vma=False)
```
